256 devices in a mesh: state: 16 (over x, y), sample: 16 (over z, core).
Axes of the slice: x: 4, y: 4, z: 8, core: 2. Of those that a mesh axis runs over, the one named last changes fastest.
Arguments:
- energy: bfloat16 [32, 524288], P(None, 'sample'), may hold values from -28 to 28
- coef: bfloat16 [32, 4096], P(None, 'state'), may hold values from -6 to 6
- anchor: int32 [524288], P('sample'), may hold values from 0 to 4096, as said below
- f_start: float32 [4096], P('state'), may hold values from -8 to 8
Outputs:
- free_energy: float32 [4096], P('state')
The draws below stay inside these ranges and needn't reach their ends.
Inputs may be any that keep to these rules, and one draw needn't show every extreme that they name: anchor_n is the state whose evolution drew slot n; the value 4096 marks an empty slot. On each index of the sample axis the live slots come first among its 32768 slots; all indices together hold exactly 196608 live slots, and on some index all 32768 slots are live. Every state is the anchor of at least one live slot.
All inputs are finite; a program needn't handle non-finite values.
Results may differ from the reference program's by a relative error of at most 0.0003.
Values may be sent and summed in bfloat16 or wider, within the bound.
No kernel may reach another device: no remote copies, remote signals or barrier semaphores. Data moves between devices by JAX's collectives and lax.ppermute only.
A program may use at most 64 MiB of HBM per device.

```python
import jax
import jax.numpy as jnp
from jax import lax

COMPONENTS = 32
SLOTS = 32768
ITERS = 2
STATES = 4096
SAMPLE_BLOCKS = 16
SAMPLES = 524288


def draw_energy(key, part):
    key_values = jax.random.fold_in(key, 3)
    values = jax.random.truncated_normal(key_values, -6.0, 6.0, (COMPONENTS, SAMPLES), jnp.float32)
    return values.astype(jnp.bfloat16)


def draw_anchor(key, part):
    key_order = jax.random.fold_in(key, 11)
    key_spread = jax.random.fold_in(key, 13)
    key_cover = jax.random.fold_in(key, 17)
    key_first = jax.random.fold_in(key, 19)
    key_second = jax.random.fold_in(key, 23)
    key_third = jax.random.fold_in(key, 29)
    blocks = SAMPLE_BLOCKS
    slot_count = SLOTS
    order = jax.random.permutation(key_order, blocks)
    position = jnp.arange(blocks, dtype=jnp.int32)
    spread = jax.random.randint(key_spread, (blocks,), 0, 5 * slot_count // 16 + 1)
    pair_index = jnp.clip((position - 3) // 2, 0, blocks - 1)
    paired = jnp.take(spread, pair_index)
    pairs_used = (blocks - 3) // 2
    signed = jnp.where((position - 3) % 2 == 0, paired, -paired)
    offset_by = jnp.where(position == 0, 5 * slot_count // 8, jnp.where(position < 3, -(5 * slot_count // 16), jnp.where(position - 3 < 2 * pairs_used, signed, 0)))
    live_by_rank = (3 * slot_count // 8 + offset_by).astype(jnp.int32)
    live_by_device = jnp.zeros((blocks,), jnp.int32).at[order].set(live_by_rank)
    first_rank = jnp.cumsum(live_by_device) - live_by_device
    slot_index = jnp.arange(SAMPLES, dtype=jnp.int32)
    device = slot_index // slot_count
    within = slot_index % slot_count
    is_live = within < jnp.take(live_by_device, device)
    live_rank = jnp.take(first_rank, device) + within
    covering = jax.random.permutation(key_cover, STATES).astype(jnp.int32)
    skewed = jnp.minimum(jax.random.randint(key_first, (SAMPLES,), 0, STATES), jnp.minimum(jax.random.randint(key_second, (SAMPLES,), 0, STATES), jax.random.randint(key_third, (SAMPLES,), 0, STATES)))
    chosen = jnp.where(live_rank < STATES, jnp.take(covering, jnp.clip(live_rank, 0, STATES - 1)), skewed)
    return jnp.where(is_live, chosen, STATES).astype(jnp.int32)


def levels(rng, dims, cuts, least, top_value):
    gain = 1.0
    for axis_at, blocks in cuts:
        heights = jax.random.uniform(jax.random.fold_in(jax.random.fold_in(rng, 6), axis_at), (blocks,), jnp.float32, least / len(cuts), top_value / len(cuts))
        gain = gain * jnp.repeat(jnp.exp(heights), dims[axis_at] // blocks).reshape((-1,) + (1,) * (len(dims) - 1 - axis_at))
    return gain


def bell_draw(rng, shape, deviation, limit, shards=(), kind=jnp.bfloat16):
    values = jax.random.normal(rng, shape, jnp.float32) * deviation
    if len(shards) > 0:
        values = levels(rng, shape, shards, -0.22, 0.18) * values
    return jnp.clip(values, min=-limit, max=limit).astype(kind)


def setup_inputs(seed: int = 0) -> dict:
    key_list = jax.random.split(jax.random.key(seed), 5)
    energy = draw_energy(jax.random.fold_in(key_list[4], 71), 0)
    coef = bell_draw(key_list[1], (COMPONENTS, STATES), 1.0, 6.0, ((1, 16),))
    anchor = draw_anchor(jax.random.fold_in(key_list[4], 71), 0)
    f_start = bell_draw(key_list[3], (STATES,), 2.0, 8.0, ((0, 16),), jnp.float32)
    return {"energy": energy, "coef": coef, "anchor": anchor, "f_start": f_start}


low_value = -1.0e30


def reference(energy, coef, anchor, f_start):
    live_mask = anchor < STATES
    histogram = jax.ops.segment_sum(jnp.ones(anchor.shape, jnp.float32), anchor, num_segments=STATES + 1)
    log_counts = jnp.log(histogram[:STATES])
    tile_len = SLOTS // 8
    tile_count = SAMPLES // tile_len
    tiles = jnp.moveaxis(energy.reshape(COMPONENTS, tile_count, tile_len), 1, 0)
    masks = live_mask.reshape(tile_count, tile_len)
    estimate = f_start
    for iteration in range(ITERS):
        log_weight = log_counts + estimate

        def visit(running, pieces):
            tile_data, tile_live = pieces
            potential = lax.dot_general(coef, tile_data, (((0,), (0,)), ((), ())), preferred_element_type=jnp.float32)
            scores = log_weight[:, None] - potential
            highest = jnp.max(scores, axis=0)
            log_denom = highest + jnp.log(jnp.sum(jnp.exp(scores - highest[None, :]), axis=0))
            weighted = jnp.where(tile_live[None, :], -potential - log_denom[None, :], low_value)
            row_high = jnp.max(weighted, axis=1)
            row_sum = jnp.sum(jnp.where(tile_live[None, :], jnp.exp(weighted - row_high[:, None]), 0.0), axis=1)
            merged = jnp.maximum(running[0], row_high)
            summed = running[1] * jnp.exp(running[0] - merged) + row_sum * jnp.exp(row_high - merged)
            return (merged, summed), None

        initial = (jnp.full((STATES,), low_value, jnp.float32), jnp.zeros((STATES,), jnp.float32))
        (highest_all, summed_all), unused_out = lax.scan(visit, initial, (tiles, masks))
        unshifted = -(highest_all + jnp.log(summed_all))
        estimate = unshifted - jnp.mean(unshifted)
    return estimate
```

```python
import functools

import jax
import jax.numpy as jnp
from jax import lax
from jax.experimental import pallas as pl
from jax.experimental.pallas import tpu as pltpu
from jax.sharding import PartitionSpec as P

ITERS = 2

LOG2E = 1.4426950408889634
LN2 = 0.6931471805599453
LOW = -1.0e30
SAFE_SUM = 1.0e-25

LANES = 128
STATE_TILE = 256
SAMPLE_TILE = 512
DEPTH = 128


def split3(value):
    high = value.astype(jnp.bfloat16).astype(jnp.float32)
    rest = value - high
    middle = rest.astype(jnp.bfloat16).astype(jnp.float32)
    low = (rest - middle).astype(jnp.bfloat16).astype(jnp.float32)
    return high, middle, low


def histogram_kernel(group_ref, anchor_ref, out_ref):
    base = group_ref[0] * 16
    total = anchor_ref.shape[1]
    step = 4096
    row = lax.broadcasted_iota(jnp.int32, (16, step), 0)
    counts = jnp.zeros((16, 16), jnp.float32)
    for start in range(0, total, step):
        anchor = anchor_ref[:, start : start + step]
        high = lax.shift_right_logical(anchor, 4) - base
        low = lax.bitwise_and(anchor, 15)
        high_hot = jnp.where(row == high, 1.0, 0.0).astype(jnp.bfloat16)
        low_hot = jnp.where(row == low, 1.0, 0.0).astype(jnp.bfloat16)
        counts += lax.dot_general(
            high_hot, low_hot, (((1,), (1,)), ((), ())), preferred_element_type=jnp.float32
        )
    lane = lax.broadcasted_iota(jnp.int32, (16, 256), 1)
    row16 = lax.broadcasted_iota(jnp.int32, (16, 256), 0)
    spread = jnp.where(lax.bitwise_and(lane, 15) == row16, 1.0, 0.0)
    placed = lax.dot_general(
        counts,
        spread,
        (((1,), (0,)), ((), ())),
        preferred_element_type=jnp.float32,
        precision=lax.Precision.HIGHEST,
    )
    flat = jnp.sum(jnp.where(lax.shift_right_logical(lane, 4) == row16, placed, 0.0), axis=0, keepdims=True)
    out_ref[...] = jnp.broadcast_to(flat[None], out_ref.shape)


def histogram(group, anchor, copies):
    total = anchor.shape[0]
    return pl.pallas_call(
        histogram_kernel,
        out_shape=jax.ShapeDtypeStruct((copies, 1, 256), jnp.float32),
        grid_spec=pltpu.PrefetchScalarGridSpec(
            num_scalar_prefetch=1,
            grid=(1,),
            in_specs=[pl.BlockSpec((1, total), lambda i, g: (0, 0))],
            out_specs=pl.BlockSpec((copies, 1, 256), lambda i, g: (0, 0, 0)),
        ),
        name="histogram",
    )(group, anchor.reshape(1, total))


def pack_kernel(counts_ref, start_ref, coef_ref, out_ref):
    counts = jnp.sum(counts_ref[...], axis=0)
    log_counts = jnp.log(counts)
    rows = list(split3(log_counts)) + list(split3(start_ref[...]))
    rows.append(jnp.zeros((2,) + counts.shape[1:], jnp.float32))
    packed = jnp.concatenate([coef_ref[...].astype(jnp.float32)] + rows, axis=0).astype(jnp.bfloat16)
    out_ref[...] = jnp.broadcast_to(packed[None], out_ref.shape)


def pack(counts, f_start, coef, copies):
    components, states = coef.shape
    return pl.pallas_call(
        pack_kernel,
        out_shape=jax.ShapeDtypeStruct((copies, components + 8, states), jnp.bfloat16),
        name="pack",
    )(counts, f_start.reshape(1, states), coef)


def merge_logs(parts):
    highest = jnp.max(parts, axis=0)
    return highest + jnp.log2(jnp.sum(jnp.exp2(parts - highest[None]), axis=0))


def merge_kernel(parts_ref, out_ref):
    out_ref[...] = jnp.broadcast_to(merge_logs(parts_ref[...])[None], out_ref.shape)


def merge(parts, copies):
    return pl.pallas_call(
        merge_kernel,
        out_shape=jax.ShapeDtypeStruct((copies,) + parts.shape[1:], jnp.float32),
        name="merge",
    )(parts)


def centered(value):
    mean = jnp.sum(jnp.sum(value, axis=1, keepdims=True), axis=0, keepdims=True) / value.size
    return value - mean


def sweep_kernel(
    first,
    group_ref,
    packed_ref,
    energy_ref,
    anchor_ref,
    *rest,
):
    if first:
        part_ref, wide_ref, column_ref, left_ref, right_ref, weight_ref, scaled_ref, high_ref, norm_ref, acc_ref, top_ref = rest
    else:
        parts_ref, old_ref, part_ref, wide_ref, column_ref, left_ref, right_ref, weight_ref, scaled_ref, high_ref, norm_ref, acc_ref, top_ref = rest
    groups = packed_ref.shape[0]
    components = energy_ref.shape[0]
    samples = energy_ref.shape[1]
    states = groups * STATE_TILE
    pair = STATE_TILE // LANES

    for g in range(groups):
        rows = packed_ref[g, components:, :].astype(jnp.float32)
        log_counts = rows[0:1] + rows[1:2] + rows[2:3]
        start = rows[3:4] + rows[4:5] + rows[5:6]
        for h in range(pair):
            at = pair * g + h
            lanes = slice(h * LANES, (h + 1) * LANES)
            column_ref[at : at + 1, :] = log_counts[:, lanes]
            if first:
                wide_ref[at : at + 1, :] = log_counts[:, lanes] + start[:, lanes]
    if not first:
        raw = old_ref[...] - merge_logs(parts_ref[...]) * LN2
        wide_ref[...] = column_ref[...] + centered(raw)

    for g in range(groups):
        coef = packed_ref[g, :components, :].astype(jnp.float32) * (-LOG2E)
        both = [wide_ref[pair * g + h : pair * g + h + 1, :] for h in range(pair)]
        weight = jnp.concatenate(both, axis=1) * LOG2E
        w0, w1, w2 = split3(weight)
        row = lax.broadcasted_iota(jnp.int32, (DEPTH - 3 * components, STATE_TILE), 0)
        tail = jnp.where(row == 0, w0, jnp.where(row == 1, w1, jnp.where(row == 2, w2, 0.0)))
        block = jnp.concatenate(list(split3(coef)) + [tail], axis=0)
        left_ref[g * STATE_TILE : (g + 1) * STATE_TILE, :] = block.T.astype(jnp.bfloat16)
    for k in range(3):
        right_ref[k * components : (k + 1) * components, :] = energy_ref[...]
    row = lax.broadcasted_iota(jnp.int32, (DEPTH - 3 * components, samples), 0)
    right_ref[3 * components :, :] = jnp.where(row < 3, 1.0, 0.0).astype(jnp.bfloat16)

    live = anchor_ref[...] < states
    weight_ref[...] = jnp.where(live, 1.0, 0.0)

    def scores(g, tile):
        return lax.dot_general(
            left_ref[g * STATE_TILE : (g + 1) * STATE_TILE, :] if isinstance(g, int) else left_ref[pl.ds(pl.multiple_of(g * STATE_TILE, STATE_TILE), STATE_TILE), :],
            right_ref[:, tile],
            (((1,), (0,)), ((), ())),
            preferred_element_type=jnp.float32,
        )

    tiles = samples // SAMPLE_TILE
    for t in range(tiles):
        tile = slice(t * SAMPLE_TILE, (t + 1) * SAMPLE_TILE)
        high = jnp.full((1, SAMPLE_TILE), LOW, jnp.float32)
        total = jnp.zeros((1, SAMPLE_TILE), jnp.float32)
        for g in range(groups):
            score = scores(g, tile)
            newer = jnp.maximum(high, jnp.max(score, axis=0, keepdims=True))
            scaled = jnp.exp2(score - newer)
            scaled_ref[g * STATE_TILE : (g + 1) * STATE_TILE, :] = scaled
            total = total * jnp.exp2(high - newer) + jnp.sum(scaled, axis=0, keepdims=True)
            high = newer
            high_ref[g : g + 1, :] = high
        norm_ref[:, tile] = high + jnp.log2(total)
        share = weight_ref[:, tile] / total
        for g in range(groups):
            factor = share * jnp.exp2(high_ref[g : g + 1, :] - high)
            part = scaled_ref[g * STATE_TILE : (g + 1) * STATE_TILE, :] * factor
            folded = part[:, :LANES]
            for k in range(1, SAMPLE_TILE // LANES):
                folded += part[:, k * LANES : (k + 1) * LANES]
            rows = slice(g * STATE_TILE, (g + 1) * STATE_TILE)
            if t == 0:
                acc_ref[rows, :] = folded
            else:
                acc_ref[rows, :] += folded

    diagonal = lax.broadcasted_iota(jnp.int32, (LANES, LANES), 0) == lax.broadcasted_iota(
        jnp.int32, (LANES, LANES), 1
    )

    def to_lanes(column):
        return jnp.sum(jnp.where(diagonal, column, 0.0), axis=0, keepdims=True)

    for k in range(states // LANES):
        rows = slice(k * LANES, (k + 1) * LANES)
        column_ref[k : k + 1, :] = to_lanes(jnp.sum(acc_ref[rows, :], axis=1, keepdims=True))
    sums = column_ref[...]
    some_live = jnp.max(weight_ref[...]) > 0.0
    result = jnp.where(sums > 0.0, jnp.log2(jnp.maximum(sums, SAFE_SUM)), LOW)
    part_ref[...] = jnp.broadcast_to(result[None], part_ref.shape)

    @pl.when(jnp.logical_and(some_live, jnp.min(sums) < SAFE_SUM))
    def exact():
        acc_ref[...] = jnp.zeros_like(acc_ref)
        top_ref[...] = jnp.full_like(top_ref, LOW)

        def visit(step, carry):
            g = step // (samples // LANES)
            at = pl.multiple_of((step % (samples // LANES)) * LANES, LANES)
            tile = pl.ds(at, LANES)
            rows = pl.ds(pl.multiple_of(g * STATE_TILE, STATE_TILE), STATE_TILE)
            is_live = weight_ref[:, tile] > 0.0
            term = jnp.where(is_live, scores(g, tile) - norm_ref[:, tile], LOW)
            older = top_ref[rows, :]
            newer = jnp.maximum(older, term)
            added = jnp.where(is_live, jnp.exp2(term - newer), 0.0)
            acc_ref[rows, :] = acc_ref[rows, :] * jnp.exp2(older - newer) + added
            top_ref[rows, :] = newer
            return carry

        lax.fori_loop(0, groups * (samples // LANES), visit, 0)
        for k in range(states // LANES):
            rows = slice(k * LANES, (k + 1) * LANES)
            top = jnp.max(top_ref[rows, :], axis=1, keepdims=True)
            total = jnp.sum(acc_ref[rows, :] * jnp.exp2(top_ref[rows, :] - top), axis=1, keepdims=True)
            value = to_lanes(top + jnp.log2(total))
            part_ref[:, k : k + 1, :] = jnp.broadcast_to(value[None], (part_ref.shape[0], 1, LANES))


def sweep(group, packed, energy, anchor, parts, old, copies):
    groups, packed_rows, _ = packed.shape
    components, columns = energy.shape
    states = groups * STATE_TILE
    share = columns // groups
    first = parts is None
    tall = states // LANES
    operands = [packed, energy, anchor.reshape(1, columns)]
    in_specs = [
        pl.BlockSpec(packed.shape, lambda i, g: (0, 0, 0)),
        pl.BlockSpec((components, share), lambda i, g: (0, g[0])),
        pl.BlockSpec((1, share), lambda i, g: (0, g[0])),
    ]
    if not first:
        operands += [parts, old]
        in_specs += [
            pl.BlockSpec(parts.shape, lambda i, g: (0, 0, 0)),
            pl.BlockSpec(old.shape, lambda i, g: (0, 0)),
        ]
    return pl.pallas_call(
        functools.partial(sweep_kernel, first),
        out_shape=[
            jax.ShapeDtypeStruct((copies, tall, LANES), jnp.float32),
            jax.ShapeDtypeStruct((tall, LANES), jnp.float32),
        ],
        grid_spec=pltpu.PrefetchScalarGridSpec(
            num_scalar_prefetch=1,
            grid=(1,),
            in_specs=in_specs,
            out_specs=[
                pl.BlockSpec((copies, tall, LANES), lambda i, g: (0, 0, 0)),
                pl.BlockSpec((tall, LANES), lambda i, g: (0, 0)),
            ],
            scratch_shapes=[
                pltpu.VMEM((tall, LANES), jnp.float32),
                pltpu.VMEM((states, DEPTH), jnp.bfloat16),
                pltpu.VMEM((DEPTH, share), jnp.bfloat16),
                pltpu.VMEM((1, share), jnp.float32),
                pltpu.VMEM((states, SAMPLE_TILE), jnp.float32),
                pltpu.VMEM((groups, SAMPLE_TILE), jnp.float32),
                pltpu.VMEM((1, share), jnp.float32),
                pltpu.VMEM((states, LANES), jnp.float32),
                pltpu.VMEM((states, LANES), jnp.float32),
            ],
        ),
        compiler_params=pltpu.CompilerParams(vmem_limit_bytes=40 * 2**20),
        name="sweep",
    )(group, *operands)


def finish_kernel(group_ref, parts_ref, old_ref, out_ref, hold_ref):
    raw = old_ref[...] - merge_logs(parts_ref[...]) * LN2
    hold_ref[...] = centered(raw)
    out_ref[...] = hold_ref[pl.ds(group_ref[0] * out_ref.shape[0], out_ref.shape[0]), :]


def finish(group, parts, old):
    rows = old.shape[0] // parts.shape[0]
    return pl.pallas_call(
        finish_kernel,
        out_shape=jax.ShapeDtypeStruct((rows, LANES), jnp.float32),
        grid_spec=pltpu.PrefetchScalarGridSpec(
            num_scalar_prefetch=1,
            grid=(1,),
            in_specs=[
                pl.BlockSpec(parts.shape, lambda i, g: (0, 0, 0)),
                pl.BlockSpec(old.shape, lambda i, g: (0, 0)),
            ],
            out_specs=pl.BlockSpec((rows, LANES), lambda i, g: (0, 0)),
            scratch_shapes=[pltpu.VMEM(old.shape, jnp.float32)],
        ),
        name="finish",
    )(group, parts, old)


def spread(copies, axis):
    return lax.all_to_all(copies, axis, 0, 0)


def per_device(energy, coef, anchor, f_start):
    groups = lax.axis_size("state")
    blocks = lax.axis_size("sample")
    group = lax.axis_index("state").astype(jnp.int32).reshape(1)
    counts = spread(histogram(group, anchor, blocks), "sample")
    packed = spread(pack(counts, f_start, coef, groups), "state")
    parts = None
    weights = None
    for iteration in range(ITERS):
        part, weights = sweep(group, packed, energy, anchor, parts, weights, blocks)
        parts = spread(merge(spread(part, "sample"), groups), "state")
    return finish(group, parts, weights).reshape(-1)


def solution(mesh):
    in_specs = (P(None, "sample"), P(None, "state"), P("sample"), P("state"))
    out_specs = P("state")
    return jax.shard_map(
        per_device, mesh=mesh, in_specs=in_specs, out_specs=out_specs, check_vma=False
    )
```

```python
import functools

import jax
import jax.numpy as jnp
from jax import lax
from jax.experimental import pallas as pl
from jax.experimental.pallas import tpu as pltpu
from jax.sharding import PartitionSpec as P

ITERS = 2

LOG2E = 1.4426950408889634
LN2 = 0.6931471805599453
LOW = -1.0e30
SAFE_SUM = 1.0e-25
SAFE_TOP = 1.0e30

LANES = 128
STATE_TILE = 256
ROW_TILE = 512
DEPTH = 128
WEIGHT_AT = 96
SHIFT_AT = 99
LIVE_AT = 102


def split3(value):
    high = value.astype(jnp.bfloat16).astype(jnp.float32)
    rest = value - high
    middle = rest.astype(jnp.bfloat16).astype(jnp.float32)
    low = (rest - middle).astype(jnp.bfloat16).astype(jnp.float32)
    return high, middle, low


def prepare_kernel(group_ref, anchor_ref, own_ref, energy_ref, out_ref, left_ref):
    base = group_ref[0] * 16
    total = anchor_ref.shape[1]
    step = 4096
    row = lax.broadcasted_iota(jnp.int32, (16, step), 0)
    counts = jnp.zeros((16, 16), jnp.float32)
    for start in range(0, total, step):
        anchor = anchor_ref[:, start : start + step]
        high = lax.shift_right_logical(anchor, 4) - base
        low = lax.bitwise_and(anchor, 15)
        high_hot = jnp.where(row == high, 1.0, 0.0).astype(jnp.bfloat16)
        low_hot = jnp.where(row == low, 1.0, 0.0).astype(jnp.bfloat16)
        counts += lax.dot_general(
            high_hot, low_hot, (((1,), (1,)), ((), ())), preferred_element_type=jnp.float32
        )
    lane = lax.broadcasted_iota(jnp.int32, (16, 256), 1)
    row16 = lax.broadcasted_iota(jnp.int32, (16, 256), 0)
    spread_out = jnp.where(lax.bitwise_and(lane, 15) == row16, 1.0, 0.0)
    placed = lax.dot_general(
        counts,
        spread_out,
        (((1,), (0,)), ((), ())),
        preferred_element_type=jnp.float32,
        precision=lax.Precision.HIGHEST,
    )
    flat = jnp.sum(jnp.where(lax.shift_right_logical(lane, 4) == row16, placed, 0.0), axis=0, keepdims=True)
    out_ref[...] = jnp.broadcast_to(flat[None], out_ref.shape)

    components, samples = energy_ref.shape
    live = jnp.where(own_ref[...] < 16 * 256, 1.0, 0.0)
    energy = energy_ref[...].astype(jnp.float32) * live
    row = lax.broadcasted_iota(jnp.int32, (DEPTH - 3 * components, samples), 0)
    ones = row < SHIFT_AT - WEIGHT_AT
    tail = jnp.where(ones, 1.0, jnp.where(row == LIVE_AT - WEIGHT_AT, live, 0.0))
    block = jnp.concatenate([energy, energy, energy, tail], axis=0)
    for at in range(0, samples, 256):
        left_ref[at : at + 256, :] = block[:, at : at + 256].T.astype(jnp.bfloat16)


def prepare(group, anchor, energy, copies, groups):
    total = anchor.shape[0]
    components = energy.shape[0]
    share = total // groups
    row = anchor.reshape(1, total)
    return pl.pallas_call(
        prepare_kernel,
        out_shape=[
            jax.ShapeDtypeStruct((copies, 1, 256), jnp.float32),
            jax.ShapeDtypeStruct((share, DEPTH), jnp.bfloat16),
        ],
        grid_spec=pltpu.PrefetchScalarGridSpec(
            num_scalar_prefetch=1,
            grid=(1,),
            in_specs=[
                pl.BlockSpec((1, total), lambda i, g: (0, 0)),
                pl.BlockSpec((1, share), lambda i, g: (0, g[0])),
                pl.BlockSpec((components, share), lambda i, g: (0, g[0])),
            ],
            out_specs=[
                pl.BlockSpec((copies, 1, 256), lambda i, g: (0, 0, 0)),
                pl.BlockSpec((share, DEPTH), lambda i, g: (0, 0)),
            ],
        ),
        name="prepare",
    )(group, row, row, energy)


def pack_kernel(counts_ref, start_ref, coef_ref, out_ref):
    counts = jnp.sum(counts_ref[...], axis=0)
    log_counts = jnp.log(counts)
    rows = list(split3(log_counts)) + list(split3(start_ref[...]))
    rows.append(jnp.zeros((2,) + counts.shape[1:], jnp.float32))
    packed = jnp.concatenate([coef_ref[...].astype(jnp.float32)] + rows, axis=0).astype(jnp.bfloat16)
    out_ref[...] = jnp.broadcast_to(packed[None], out_ref.shape)


def pack(counts, f_start, coef, copies):
    components, states = coef.shape
    return pl.pallas_call(
        pack_kernel,
        out_shape=jax.ShapeDtypeStruct((copies, components + 8, states), jnp.bfloat16),
        name="pack",
    )(counts, f_start.reshape(1, states), coef)


def merge_logs(parts):
    highest = jnp.max(parts, axis=0)
    return highest + jnp.log2(jnp.sum(jnp.exp2(parts - highest[None]), axis=0))


def merge_kernel(parts_ref, out_ref):
    out_ref[...] = jnp.broadcast_to(merge_logs(parts_ref[...])[None], out_ref.shape)


def merge(parts, copies):
    return pl.pallas_call(
        merge_kernel,
        out_shape=jax.ShapeDtypeStruct((copies,) + parts.shape[1:], jnp.float32),
        name="merge",
    )(parts)


def centered(value):
    mean = jnp.sum(jnp.sum(value, axis=1, keepdims=True), axis=0, keepdims=True) / value.size
    return value - mean


def largest(value):
    return jnp.max(jnp.max(value, axis=1, keepdims=True), axis=0, keepdims=True)


def folded(value, combine):
    return combine(value[:, :LANES], value[:, LANES:])


def sweep_kernel(first, *refs):
    if first:
        packed_ref, left_ref, part_ref, wide_ref, shifted_ref, right_ref, scaled_ref, acc_ref, some_ref, norm_ref, top_ref = refs
        source_ref = shifted_ref
    else:
        packed_ref, left_ref, parts_ref, old_ref, part_ref, wide_ref, some_ref, right_ref, scaled_ref, acc_ref, norm_ref, top_ref = refs
        source_ref = left_ref
    groups, packed_rows, _ = packed_ref.shape
    components = packed_rows - 8
    samples = left_ref.shape[0]
    states = groups * STATE_TILE
    pair = STATE_TILE // LANES
    tiles = samples // ROW_TILE

    for g in range(groups):
        rows = packed_ref[g, components:, :].astype(jnp.float32)
        log_counts = rows[0:1] + rows[1:2] + rows[2:3]
        value = log_counts + (rows[3:4] + rows[4:5] + rows[5:6]) if first else log_counts
        for h in range(pair):
            wide_ref[pair * g + h : pair * g + h + 1, :] = value[:, h * LANES : (h + 1) * LANES]
    if first:
        weights = wide_ref[...]
    else:
        raw = old_ref[...] - merge_logs(parts_ref[...]) * LN2
        wide = wide_ref[...] + centered(raw)
        wide_ref[...] = wide
        weights = wide - largest(wide - old_ref[...])
    w0, w1, w2 = split3(weights * LOG2E)

    row = lax.broadcasted_iota(jnp.int32, (DEPTH - 3 * components, LANES), 0)
    ones = jnp.where(row < LIVE_AT - WEIGHT_AT, 1.0, 0.0)
    for g in range(groups):
        coef = packed_ref[g, :components, :].astype(jnp.float32) * (-LOG2E)
        lanes = slice(g * STATE_TILE, (g + 1) * STATE_TILE)
        for k, part in enumerate(split3(coef)):
            right_ref[k * components : (k + 1) * components, lanes] = part.astype(jnp.bfloat16)
        for h in range(pair):
            at = pair * g + h
            tail = jnp.where(row == 0, w0[at : at + 1], jnp.where(row == 1, w1[at : at + 1], jnp.where(row == 2, w2[at : at + 1], ones)))
            right_ref[WEIGHT_AT:, at * LANES : (at + 1) * LANES] = tail.astype(jnp.bfloat16)

    def product(left, right):
        return lax.dot_general(left, right, (((1,), (0,)), ((), ())), preferred_element_type=jnp.float32)

    if first:
        lane = lax.broadcasted_iota(jnp.int32, (DEPTH, LANES), 1)
        for h in range(2):
            some = jnp.zeros((DEPTH, LANES), jnp.float32)
            for j in range(8):
                g = 8 * h + j
                tile = right_ref[:, g * STATE_TILE : g * STATE_TILE + LANES].astype(jnp.float32)
                moved = tile if j == 0 else pltpu.roll(tile, 16 * j, 1)
                some = jnp.where(lax.shift_right_logical(lane, 4) == j, moved, some)
            some_ref[:, h * LANES : (h + 1) * LANES] = some.astype(jnp.bfloat16)

    acc_ref[...] = jnp.zeros_like(acc_ref)
    lane = lax.broadcasted_iota(jnp.int32, (ROW_TILE, LANES), 1)

    def shifted(block, shift):
        s0, s1, s2 = split3(-shift)
        values = jnp.where(lane == SHIFT_AT, s0, jnp.where(lane == SHIFT_AT + 1, s1, s2))
        chosen = jnp.logical_and(lane >= SHIFT_AT, lane < LIVE_AT)
        return jnp.where(chosen, values, block.astype(jnp.float32)).astype(jnp.bfloat16)

    def visit(t, carry):
        least, most = carry
        rows = pl.ds(pl.multiple_of(t * ROW_TILE, ROW_TILE), ROW_TILE)
        left = left_ref[rows, :]
        if first:
            sampled = folded(product(left, some_ref[...]), jnp.maximum)
            shift = jnp.max(sampled, axis=1, keepdims=True)
            left = shifted(left, shift)
        live = left_ref[rows, LIVE_AT : LIVE_AT + 1].astype(jnp.float32)
        total = jnp.zeros((ROW_TILE, LANES), jnp.float32)
        for g in range(groups):
            lanes = slice(g * STATE_TILE, (g + 1) * STATE_TILE)
            scaled = jnp.exp2(product(left, right_ref[:, lanes]))
            scaled_ref[:, lanes] = scaled
            total += folded(scaled, jnp.add)
        denominator = jnp.sum(total, axis=1, keepdims=True)
        least = jnp.minimum(least, jnp.where(live > 0.0, denominator, 1.0))
        most = jnp.maximum(most, jnp.where(live > 0.0, denominator, 1.0))
        share = jnp.broadcast_to(live / denominator, (ROW_TILE, LANES))
        if first:
            shifted_ref[rows, :] = shifted(left, shift + jnp.log2(denominator))
        for k in range(states // LANES):
            lanes = slice(k * LANES, (k + 1) * LANES)
            part = scaled_ref[:, lanes] * share
            acc_ref[:, lanes] += jnp.sum(part.reshape(ROW_TILE // 8, 8, LANES), axis=0)
        return least, most

    unit = jnp.ones((ROW_TILE, 1), jnp.float32)
    least, most = lax.fori_loop(0, tiles, visit, (unit, unit))
    least = jnp.min(least)
    most = jnp.max(most)
    sums = jnp.sum(acc_ref[...], axis=0, keepdims=True)
    smallest = jnp.min(sums)
    some_live = jnp.max(left_ref[:, LIVE_AT : LIVE_AT + 1].astype(jnp.float32)) > 0.0
    logs = jnp.where(sums > 0.0, jnp.log2(jnp.maximum(sums, SAFE_SUM)), LOW)

    def give(value):
        for k in range(states // LANES):
            piece = value[:, k * LANES : (k + 1) * LANES]
            part_ref[:, k : k + 1, :] = jnp.broadcast_to(piece[None], (part_ref.shape[0], 1, LANES))

    give(logs)
    enough = jnp.logical_and(smallest >= SAFE_SUM, smallest * least >= SAFE_SUM)
    safe = jnp.logical_and(enough, jnp.logical_and(most < SAFE_TOP, least > SAFE_SUM))

    @pl.when(jnp.logical_and(some_live, jnp.logical_not(safe)))
    def exact():
        acc_ref[...] = jnp.zeros_like(acc_ref)
        top_ref[...] = jnp.full_like(top_ref, LOW)

        def tile_at(k):
            return pl.ds(pl.multiple_of(k * LANES, LANES), LANES)

        def slots(t, carry):
            rows = pl.ds(pl.multiple_of(t * ROW_TILE, ROW_TILE), ROW_TILE)
            left = left_ref[rows, :]
            is_live = jnp.broadcast_to(left[:, LIVE_AT : LIVE_AT + 1].astype(jnp.float32), (ROW_TILE, LANES)) > 0.0

            def column(k, pieces):
                high, total = pieces
                score = product(left, right_ref[:, tile_at(k)])
                newer = jnp.maximum(high, score)
                return newer, total * jnp.exp2(high - newer) + jnp.exp2(score - newer)

            start = (jnp.full((ROW_TILE, LANES), LOW, jnp.float32), jnp.zeros((ROW_TILE, LANES), jnp.float32))
            high, total = lax.fori_loop(0, states // LANES, column, start)
            top = jnp.max(high, axis=1, keepdims=True)
            total = jnp.sum(total * jnp.exp2(high - top), axis=1, keepdims=True)
            norm = top + jnp.log2(total)
            if first:
                shifted_ref[rows, :] = shifted(left, norm)

            def state(k, inner):
                lanes = tile_at(k)
                term = jnp.where(is_live, product(left, right_ref[:, lanes]) - norm, LOW)
                older = top_ref[:, lanes]
                newer = jnp.maximum(older, jnp.max(term, axis=0, keepdims=True))
                added = jnp.sum(jnp.where(is_live, jnp.exp2(term - newer), 0.0), axis=0, keepdims=True)
                acc_ref[0:1, lanes] = acc_ref[0:1, lanes] * jnp.exp2(older - newer) + added
                top_ref[:, lanes] = newer
                return inner

            return lax.fori_loop(0, states // LANES, state, carry)

        lax.fori_loop(0, tiles, slots, 0)
        give(top_ref[...] + jnp.log2(acc_ref[0:1, :]))


def whole(shape):
    return pl.BlockSpec(shape, lambda: (0,) * len(shape))


def sweep(packed, left, parts, old, copies):
    groups = packed.shape[0]
    states = groups * STATE_TILE
    samples = left.shape[0]
    first = parts is None
    tall = states // LANES
    operands = [packed, left] + ([] if first else [parts, old])
    outs = [((copies, tall, LANES), jnp.float32), ((tall, LANES), jnp.float32)]
    scratch = [
        pltpu.VMEM((DEPTH, states), jnp.bfloat16),
        pltpu.VMEM((ROW_TILE, states), jnp.float32),
        pltpu.VMEM((8, states), jnp.float32),
        pltpu.VMEM((DEPTH, 2 * LANES), jnp.bfloat16),
        pltpu.VMEM((8, LANES), jnp.float32),
        pltpu.VMEM((1, states), jnp.float32),
    ]
    if first:
        outs.append((left.shape, jnp.bfloat16))
    else:
        scratch = [scratch[3]] + scratch[:3] + scratch[4:]
    return pl.pallas_call(
        functools.partial(sweep_kernel, first),
        out_shape=[jax.ShapeDtypeStruct(*out) for out in outs],
        scratch_shapes=scratch,
        compiler_params=pltpu.CompilerParams(vmem_limit_bytes=40 * 2**20),
        name="first_sweep" if first else "next_sweep",
    )(*operands)


def finish_kernel(group_ref, parts_ref, old_ref, out_ref, hold_ref):
    raw = old_ref[...] - merge_logs(parts_ref[...]) * LN2
    hold_ref[...] = centered(raw)
    out_ref[...] = hold_ref[pl.ds(group_ref[0] * out_ref.shape[0], out_ref.shape[0]), :]


def finish(group, parts, old):
    rows = old.shape[0] // parts.shape[0]
    return pl.pallas_call(
        finish_kernel,
        out_shape=jax.ShapeDtypeStruct((rows, LANES), jnp.float32),
        grid_spec=pltpu.PrefetchScalarGridSpec(
            num_scalar_prefetch=1,
            grid=(1,),
            in_specs=[
                pl.BlockSpec(parts.shape, lambda i, g: (0, 0, 0)),
                pl.BlockSpec(old.shape, lambda i, g: (0, 0)),
            ],
            out_specs=pl.BlockSpec((rows, LANES), lambda i, g: (0, 0)),
            scratch_shapes=[pltpu.VMEM(old.shape, jnp.float32)],
        ),
        name="finish",
    )(group, parts, old)


def spread(copies, axis):
    return lax.all_to_all(copies, axis, 0, 0)


def per_device(energy, coef, anchor, f_start):
    groups = lax.axis_size("state")
    blocks = lax.axis_size("sample")
    group = lax.axis_index("state").astype(jnp.int32).reshape(1)
    counts, left = prepare(group, anchor, energy, blocks, groups)
    counts = spread(counts, "sample")
    packed = spread(pack(counts, f_start, coef, groups), "state")
    parts = None
    weights = None
    for iteration in range(ITERS):
        part, weights, *rest = sweep(packed, left, parts, weights, blocks)
        if rest:
            left = rest[0]
        parts = spread(merge(spread(part, "sample"), groups), "state")
    return finish(group, parts, weights).reshape(-1)


def solution(mesh):
    in_specs = (P(None, "sample"), P(None, "state"), P("sample"), P("state"))
    out_specs = P("state")
    return jax.shard_map(
        per_device, mesh=mesh, in_specs=in_specs, out_specs=out_specs, check_vma=False
    )
```

```python
import functools

import jax
import jax.numpy as jnp
from jax import lax
from jax.experimental import pallas as pl
from jax.experimental.pallas import tpu as pltpu
from jax.sharding import PartitionSpec as P

ITERS = 2

LOG2E = 1.4426950408889634
LN2 = 0.6931471805599453
LOW = -1.0e30
SAFE_SUM = 1.0e-25
SAFE_TOP = 1.0e30

LANES = 128
STATE_TILE = 256
ROW_TILE = 512
DEPTH = 128
WEIGHT_AT = 96
SHIFT_AT = 99
LIVE_AT = 102


def split3(value):
    high = value.astype(jnp.bfloat16).astype(jnp.float32)
    rest = value - high
    middle = rest.astype(jnp.bfloat16).astype(jnp.float32)
    low = (rest - middle).astype(jnp.bfloat16).astype(jnp.float32)
    return high, middle, low


def live_rows(group, own, live_slots):
    lane = lax.broadcasted_iota(jnp.int32, (1, LANES), 1)
    tile = group + 16 * lax.shift_right_logical(lane, 3)
    slot = tile * LANES + 8 * own + lax.bitwise_and(lane, 7)
    return slot.astype(jnp.float32) < live_slots


def prepare_kernel(place_ref, anchor_ref, energy_ref, out_ref, tile_ref, sems):
    group = place_ref[0]
    tiles = tile_ref.shape[0]

    def fetch(i):
        at = pl.multiple_of((group + tiles * i) * LANES, LANES)
        return pltpu.make_async_copy(energy_ref.at[:, pl.ds(at, LANES)], tile_ref.at[i], sems.at[i])

    for i in range(tiles):
        fetch(i).start()
    base = group * 16
    total = anchor_ref.shape[1]
    step = 4096
    row = lax.broadcasted_iota(jnp.int32, (16, step), 0)
    counts = jnp.zeros((16, 16), jnp.float32)
    live = jnp.zeros((1, step), jnp.float32)
    for start in range(0, total, step):
        anchor = anchor_ref[:, start : start + step]
        high = lax.shift_right_logical(anchor, 4) - base
        low = lax.bitwise_and(anchor, 15)
        high_hot = jnp.where(row == high, 1.0, 0.0).astype(jnp.bfloat16)
        low_hot = jnp.where(row == low, 1.0, 0.0).astype(jnp.bfloat16)
        live += jnp.where(anchor < tiles * STATE_TILE, 1.0, 0.0)
        counts += lax.dot_general(
            high_hot, low_hot, (((1,), (1,)), ((), ())), preferred_element_type=jnp.float32
        )
    lane = lax.broadcasted_iota(jnp.int32, (16, 256), 1)
    row16 = lax.broadcasted_iota(jnp.int32, (16, 256), 0)
    spread_out = jnp.where(lax.bitwise_and(lane, 15) == row16, 1.0, 0.0)
    placed = lax.dot_general(
        counts,
        spread_out,
        (((1,), (0,)), ((), ())),
        preferred_element_type=jnp.float32,
        precision=lax.Precision.HIGHEST,
    )
    flat = jnp.sum(jnp.where(lax.shift_right_logical(lane, 4) == row16, placed, 0.0), axis=0, keepdims=True)
    amount = jnp.broadcast_to(jnp.sum(live, axis=1, keepdims=True), (1, LANES))

    def halves(value):
        high = jnp.floor(value * (1.0 / 256.0))
        return high, value - high * 256.0

    flat_high, flat_low = halves(flat)
    rows = [flat_high[:, :LANES], flat_high[:, LANES:], flat_low[:, :LANES], flat_low[:, LANES:]]
    rows += list(halves(amount)) + [jnp.zeros((2, LANES), jnp.float32)]
    for i in range(tiles):
        fetch(i).wait()
    lane = lax.shift_right_logical(lax.broadcasted_iota(jnp.int32, tile_ref.shape[1:], 1), 3)
    energies = [tile_ref[i].astype(jnp.float32) for i in range(tiles)]
    for j in range(out_ref.shape[0]):
        piece = energies[j]
        for i in range(tiles):
            if i != j:
                piece = jnp.where(lane == i, pltpu.roll(energies[i], (8 * (i - j)) % LANES, 1), piece)
        out_ref[j] = jnp.concatenate([piece] + rows, axis=0).astype(jnp.bfloat16)


def prepare(place, anchor, energy, copies, groups):
    total = anchor.shape[0]
    components = energy.shape[0]
    return pl.pallas_call(
        prepare_kernel,
        out_shape=jax.ShapeDtypeStruct((copies, components + 8, LANES), jnp.bfloat16),
        grid_spec=pltpu.PrefetchScalarGridSpec(
            num_scalar_prefetch=1,
            grid=(1,),
            in_specs=[
                pl.BlockSpec((1, total), lambda i, g: (0, 0)),
                pl.BlockSpec(memory_space=pl.ANY),
            ],
            out_specs=pl.BlockSpec((copies, components + 8, LANES), lambda i, g: (0, 0, 0)),
            scratch_shapes=[
                pltpu.VMEM((groups, components, LANES), jnp.bfloat16),
                pltpu.SemaphoreType.DMA((groups,)),
            ],
        ),
        name="prepare",
    )(place, anchor.reshape(1, total), energy)


def collect_kernel(place_ref, pieces_ref, start_ref, coef_ref, out_ref, left_ref, amount_ref, wide_ref):
    components = coef_ref.shape[0]
    wide_ref[...] = jnp.zeros_like(wide_ref)
    counts = jnp.zeros((1, STATE_TILE), jnp.float32)
    lane = lax.broadcasted_iota(jnp.int32, (1, LANES), 1)
    row = lax.broadcasted_iota(jnp.int32, (DEPTH - 3 * components, LANES), 0)
    at = jnp.int32(0)
    for b in range(pieces_ref.shape[0]):
        piece = pieces_ref[b].astype(jnp.float32)
        rest = piece[components:]
        counts += jnp.concatenate([rest[0:1], rest[1:2]], axis=1) * 256.0
        counts += jnp.concatenate([rest[2:3], rest[3:4]], axis=1)
        is_live = live_rows(place_ref[0], place_ref[1], rest[4:5] * 256.0 + rest[5:6])
        live = jnp.where(is_live, 1.0, 0.0)
        starts = jnp.where(lax.bitwise_and(lane, 7) == 0, live, 0.0)
        energy = piece[:components] * live
        tail = jnp.where(row < SHIFT_AT - WEIGHT_AT, 1.0, jnp.where(row == LIVE_AT - WEIGHT_AT, live, 0.0))
        block = jnp.concatenate([energy, energy, energy, tail], axis=0)
        wide_ref[pl.ds(pl.multiple_of(at, 8), LANES), :] = block.T
        at = at + 8 * jnp.sum(starts).astype(jnp.int32)
    left_ref[...] = wide_ref[...].astype(jnp.bfloat16)
    amount_ref[0] = at
    rows = list(split3(jnp.log(counts))) + list(split3(start_ref[...]))
    rows.append(jnp.zeros((2, STATE_TILE), jnp.float32))
    packed = jnp.concatenate([coef_ref[...].astype(jnp.float32)] + rows, axis=0).astype(jnp.bfloat16)
    out_ref[...] = jnp.broadcast_to(packed[None], out_ref.shape)


def collect(place, pieces, f_start, coef, copies):
    components, states = coef.shape
    most = pieces.shape[0] * LANES
    return pl.pallas_call(
        collect_kernel,
        out_shape=[
            jax.ShapeDtypeStruct((copies, components + 8, states), jnp.bfloat16),
            jax.ShapeDtypeStruct((most, DEPTH), jnp.bfloat16),
            jax.ShapeDtypeStruct((1,), jnp.int32),
        ],
        in_specs=[pl.BlockSpec(memory_space=pltpu.SMEM)] + [pl.BlockSpec(memory_space=pltpu.VMEM)] * 3,
        out_specs=[pl.BlockSpec(memory_space=pltpu.VMEM)] * 2 + [pl.BlockSpec(memory_space=pltpu.SMEM)],
        scratch_shapes=[pltpu.VMEM((most, DEPTH), jnp.float32)],
        name="collect",
    )(place, pieces, f_start.reshape(1, states), coef)


def merge_logs(parts):
    highest = jnp.max(parts, axis=0)
    return highest + jnp.log2(jnp.sum(jnp.exp2(parts - highest[None]), axis=0))


def merge_kernel(parts_ref, out_ref):
    out_ref[...] = jnp.broadcast_to(merge_logs(parts_ref[...])[None], out_ref.shape)


def merge(parts, copies):
    return pl.pallas_call(
        merge_kernel,
        out_shape=jax.ShapeDtypeStruct((copies,) + parts.shape[1:], jnp.float32),
        name="merge",
    )(parts)


def centered(value):
    mean = jnp.sum(jnp.sum(value, axis=1, keepdims=True), axis=0, keepdims=True) / value.size
    return value - mean


def largest(value):
    return jnp.max(jnp.max(value, axis=1, keepdims=True), axis=0, keepdims=True)


def folded(value, combine):
    return combine(value[:, :LANES], value[:, LANES:])


def sweep_kernel(first, *refs):
    if first:
        amount_ref, packed_ref, left_ref, part_ref, wide_ref, shifted_ref, right_ref, scaled_ref, acc_ref, some_ref, norm_ref, top_ref = refs
        source_ref = shifted_ref
    else:
        amount_ref, packed_ref, left_ref, parts_ref, old_ref, part_ref, wide_ref, some_ref, right_ref, scaled_ref, acc_ref, norm_ref, top_ref = refs
        source_ref = left_ref
    groups, packed_rows, _ = packed_ref.shape
    components = packed_rows - 8
    states = groups * STATE_TILE
    pair = STATE_TILE // LANES
    amount = amount_ref[0]
    tiles = (amount + ROW_TILE - 1) // ROW_TILE

    for g in range(groups):
        rows = packed_ref[g, components:, :].astype(jnp.float32)
        log_counts = rows[0:1] + rows[1:2] + rows[2:3]
        value = log_counts + (rows[3:4] + rows[4:5] + rows[5:6]) if first else log_counts
        for h in range(pair):
            wide_ref[pair * g + h : pair * g + h + 1, :] = value[:, h * LANES : (h + 1) * LANES]
    if first:
        weights = wide_ref[...]
    else:
        raw = old_ref[...] - merge_logs(parts_ref[...]) * LN2
        wide = wide_ref[...] + centered(raw)
        wide_ref[...] = wide
        weights = wide - largest(wide - old_ref[...])
    w0, w1, w2 = split3(weights * LOG2E)

    row = lax.broadcasted_iota(jnp.int32, (DEPTH - 3 * components, LANES), 0)
    ones = jnp.where(row < LIVE_AT - WEIGHT_AT, 1.0, 0.0)
    for g in range(groups):
        coef = packed_ref[g, :components, :].astype(jnp.float32) * (-LOG2E)
        lanes = slice(g * STATE_TILE, (g + 1) * STATE_TILE)
        for k, part in enumerate(split3(coef)):
            right_ref[k * components : (k + 1) * components, lanes] = part.astype(jnp.bfloat16)
        for h in range(pair):
            at = pair * g + h
            tail = jnp.where(row == 0, w0[at : at + 1], jnp.where(row == 1, w1[at : at + 1], jnp.where(row == 2, w2[at : at + 1], ones)))
            right_ref[WEIGHT_AT:, at * LANES : (at + 1) * LANES] = tail.astype(jnp.bfloat16)

    def product(left, right):
        return lax.dot_general(left, right, (((1,), (0,)), ((), ())), preferred_element_type=jnp.float32)

    if first:
        lane = lax.broadcasted_iota(jnp.int32, (DEPTH, LANES), 1)
        for h in range(2):
            some = jnp.zeros((DEPTH, LANES), jnp.float32)
            for j in range(8):
                g = 8 * h + j
                tile = right_ref[:, g * STATE_TILE : g * STATE_TILE + LANES].astype(jnp.float32)
                moved = tile if j == 0 else pltpu.roll(tile, 16 * j, 1)
                some = jnp.where(lax.shift_right_logical(lane, 4) == j, moved, some)
            some_ref[:, h * LANES : (h + 1) * LANES] = some.astype(jnp.bfloat16)

    acc_ref[...] = jnp.zeros_like(acc_ref)
    lane = lax.broadcasted_iota(jnp.int32, (ROW_TILE, LANES), 1)

    def shifted(block, shift):
        s0, s1, s2 = split3(-shift)
        values = jnp.where(lane == SHIFT_AT, s0, jnp.where(lane == SHIFT_AT + 1, s1, s2))
        chosen = jnp.logical_and(lane >= SHIFT_AT, lane < LIVE_AT)
        return jnp.where(chosen, values, block.astype(jnp.float32)).astype(jnp.bfloat16)

    def visit(t, carry):
        least, most = carry
        rows = pl.ds(pl.multiple_of(t * ROW_TILE, ROW_TILE), ROW_TILE)
        left = left_ref[rows, :]
        if first:
            sampled = folded(product(left, some_ref[...]), jnp.maximum)
            shift = jnp.max(sampled, axis=1, keepdims=True)
            left = shifted(left, shift)
        live = left_ref[rows, LIVE_AT : LIVE_AT + 1].astype(jnp.float32)
        total = jnp.zeros((ROW_TILE, LANES), jnp.float32)
        for g in range(groups):
            lanes = slice(g * STATE_TILE, (g + 1) * STATE_TILE)
            scaled = jnp.exp2(product(left, right_ref[:, lanes]))
            scaled_ref[:, lanes] = scaled
            total += folded(scaled, jnp.add)
        denominator = jnp.sum(total, axis=1, keepdims=True)
        least = jnp.minimum(least, jnp.where(live > 0.0, denominator, 1.0))
        most = jnp.maximum(most, jnp.where(live > 0.0, denominator, 1.0))
        share = jnp.broadcast_to(live / denominator, (ROW_TILE, LANES))
        if first:
            shifted_ref[rows, :] = shifted(left, shift + jnp.log2(denominator))
        for k in range(states // LANES):
            lanes = slice(k * LANES, (k + 1) * LANES)
            part = scaled_ref[:, lanes] * share
            acc_ref[:, lanes] += jnp.sum(part.reshape(ROW_TILE // 8, 8, LANES), axis=0)
        return least, most

    unit = jnp.ones((ROW_TILE, 1), jnp.float32)
    least, most = lax.fori_loop(0, tiles, visit, (unit, unit))
    least = jnp.min(least)
    most = jnp.max(most)
    sums = jnp.sum(acc_ref[...], axis=0, keepdims=True)
    smallest = jnp.min(sums)
    some_live = amount > 0
    logs = jnp.where(sums > 0.0, jnp.log2(jnp.maximum(sums, SAFE_SUM)), LOW)

    def give(value):
        for k in range(states // LANES):
            piece = value[:, k * LANES : (k + 1) * LANES]
            part_ref[:, k : k + 1, :] = jnp.broadcast_to(piece[None], (part_ref.shape[0], 1, LANES))

    give(logs)
    enough = jnp.logical_and(smallest >= SAFE_SUM, smallest * least >= SAFE_SUM)
    safe = jnp.logical_and(enough, jnp.logical_and(most < SAFE_TOP, least > SAFE_SUM))

    @pl.when(jnp.logical_and(some_live, jnp.logical_not(safe)))
    def exact():
        acc_ref[...] = jnp.zeros_like(acc_ref)
        top_ref[...] = jnp.full_like(top_ref, LOW)

        def tile_at(k):
            return pl.ds(pl.multiple_of(k * LANES, LANES), LANES)

        def slots(t, carry):
            rows = pl.ds(pl.multiple_of(t * ROW_TILE, ROW_TILE), ROW_TILE)
            left = left_ref[rows, :]
            is_live = jnp.broadcast_to(left[:, LIVE_AT : LIVE_AT + 1].astype(jnp.float32), (ROW_TILE, LANES)) > 0.0

            def column(k, pieces):
                high, total = pieces
                score = product(left, right_ref[:, tile_at(k)])
                newer = jnp.maximum(high, score)
                return newer, total * jnp.exp2(high - newer) + jnp.exp2(score - newer)

            start = (jnp.full((ROW_TILE, LANES), LOW, jnp.float32), jnp.zeros((ROW_TILE, LANES), jnp.float32))
            high, total = lax.fori_loop(0, states // LANES, column, start)
            top = jnp.max(high, axis=1, keepdims=True)
            total = jnp.sum(total * jnp.exp2(high - top), axis=1, keepdims=True)
            norm = top + jnp.log2(total)
            if first:
                shifted_ref[rows, :] = shifted(left, norm)

            def state(k, inner):
                lanes = tile_at(k)
                term = jnp.where(is_live, product(left, right_ref[:, lanes]) - norm, LOW)
                older = top_ref[:, lanes]
                newer = jnp.maximum(older, jnp.max(term, axis=0, keepdims=True))
                added = jnp.sum(jnp.where(is_live, jnp.exp2(term - newer), 0.0), axis=0, keepdims=True)
                acc_ref[0:1, lanes] = acc_ref[0:1, lanes] * jnp.exp2(older - newer) + added
                top_ref[:, lanes] = newer
                return inner

            return lax.fori_loop(0, states // LANES, state, carry)

        lax.fori_loop(0, tiles, slots, 0)
        give(top_ref[...] + jnp.log2(acc_ref[0:1, :]))


def sweep(amount, packed, left, parts, old, copies):
    groups = packed.shape[0]
    states = groups * STATE_TILE
    first = parts is None
    tall = states // LANES
    operands = [amount, packed, left] + ([] if first else [parts, old])
    outs = [((copies, tall, LANES), jnp.float32), ((tall, LANES), jnp.float32)]
    scratch = [
        pltpu.VMEM((DEPTH, states), jnp.bfloat16),
        pltpu.VMEM((ROW_TILE, states), jnp.float32),
        pltpu.VMEM((8, states), jnp.float32),
        pltpu.VMEM((DEPTH, 2 * LANES), jnp.bfloat16),
        pltpu.VMEM((8, LANES), jnp.float32),
        pltpu.VMEM((1, states), jnp.float32),
    ]
    if first:
        outs.append((left.shape, jnp.bfloat16))
    else:
        scratch = [scratch[3]] + scratch[:3] + scratch[4:]
    return pl.pallas_call(
        functools.partial(sweep_kernel, first),
        out_shape=[jax.ShapeDtypeStruct(*out) for out in outs],
        in_specs=[pl.BlockSpec(memory_space=pltpu.SMEM)] + [pl.BlockSpec(memory_space=pltpu.VMEM)] * (len(operands) - 1),
        scratch_shapes=scratch,
        compiler_params=pltpu.CompilerParams(vmem_limit_bytes=40 * 2**20),
        name="first_sweep" if first else "next_sweep",
    )(*operands)


def finish_kernel(group_ref, parts_ref, old_ref, out_ref, hold_ref):
    raw = old_ref[...] - merge_logs(parts_ref[...]) * LN2
    hold_ref[...] = centered(raw)
    out_ref[...] = hold_ref[pl.ds(group_ref[0] * out_ref.shape[0], out_ref.shape[0]), :]


def finish(group, parts, old):
    rows = old.shape[0] // parts.shape[0]
    return pl.pallas_call(
        finish_kernel,
        out_shape=jax.ShapeDtypeStruct((rows, LANES), jnp.float32),
        grid_spec=pltpu.PrefetchScalarGridSpec(
            num_scalar_prefetch=1,
            grid=(1,),
            in_specs=[
                pl.BlockSpec(parts.shape, lambda i, g: (0, 0, 0)),
                pl.BlockSpec(old.shape, lambda i, g: (0, 0)),
            ],
            out_specs=pl.BlockSpec((rows, LANES), lambda i, g: (0, 0)),
            scratch_shapes=[pltpu.VMEM(old.shape, jnp.float32)],
        ),
        name="finish",
    )(group, parts, old)


def spread(copies, axis):
    return lax.all_to_all(copies, axis, 0, 0)


def per_device(energy, coef, anchor, f_start):
    groups = lax.axis_size("state")
    blocks = lax.axis_size("sample")
    place = jnp.stack([lax.axis_index("state"), lax.axis_index("sample")]).astype(jnp.int32)
    pieces = spread(prepare(place, anchor, energy, blocks, groups), "sample")
    packed, left, amount = collect(place, pieces, f_start, coef, groups)
    packed = spread(packed, "state")
    parts = None
    weights = None
    for iteration in range(ITERS):
        part, weights, *rest = sweep(amount, packed, left, parts, weights, blocks)
        if rest:
            left = rest[0]
        parts = spread(merge(spread(part, "sample"), groups), "state")
    return finish(place, parts, weights).reshape(-1)


def solution(mesh):
    in_specs = (P(None, "sample"), P(None, "state"), P("sample"), P("state"))
    out_specs = P("state")
    return jax.shard_map(
        per_device, mesh=mesh, in_specs=in_specs, out_specs=out_specs, check_vma=False
    )
```

```python
import functools

import jax
import jax.numpy as jnp
from jax import lax
from jax.experimental import pallas as pl
from jax.experimental.pallas import tpu as pltpu
from jax.sharding import PartitionSpec as P

ITERS = 2

LOG2E = 1.4426950408889634
LN2 = 0.6931471805599453
LOW = -1.0e30
SAFE_SUM = 1.0e-25
SAFE_TOP = 1.0e30

LANES = 128
STATE_TILE = 256
ROW_TILE = 416
DEPTH = 128
WEIGHT_AT = 96
SHIFT_AT = 99
LIVE_AT = 102


def split3(value):
    high = value.astype(jnp.bfloat16).astype(jnp.float32)
    rest = value - high
    middle = rest.astype(jnp.bfloat16).astype(jnp.float32)
    low = (rest - middle).astype(jnp.bfloat16).astype(jnp.float32)
    return high, middle, low


def live_rows(group, own, live_slots):
    lane = lax.broadcasted_iota(jnp.int32, (1, LANES), 1)
    tile = group + 16 * lax.shift_right_logical(lane, 3)
    slot = tile * LANES + 8 * own + lax.bitwise_and(lane, 7)
    return slot.astype(jnp.float32) < live_slots


def prepare_kernel(group_ref, anchor_ref, energy_ref, out_ref, tile_ref, sems):
    group = group_ref[0]
    tiles = tile_ref.shape[0]

    def fetch(i):
        at = pl.multiple_of((group + tiles * i) * LANES, LANES)
        return pltpu.make_async_copy(energy_ref.at[:, pl.ds(at, LANES)], tile_ref.at[i], sems.at[i])

    for i in range(tiles):
        fetch(i).start()
    base = group * 16
    total = anchor_ref.shape[1]
    step = 4096
    row = lax.broadcasted_iota(jnp.int32, (16, step), 0)
    counts = jnp.zeros((16, 16), jnp.float32)
    live = jnp.zeros((1, step), jnp.float32)
    for start in range(0, total, step):
        anchor = anchor_ref[:, start : start + step]
        high = lax.shift_right_logical(anchor, 4) - base
        low = lax.bitwise_and(anchor, 15)
        high_hot = jnp.where(row == high, 1.0, 0.0).astype(jnp.bfloat16)
        low_hot = jnp.where(row == low, 1.0, 0.0).astype(jnp.bfloat16)
        live += jnp.where(anchor < tiles * STATE_TILE, 1.0, 0.0)
        counts += lax.dot_general(
            high_hot, low_hot, (((1,), (1,)), ((), ())), preferred_element_type=jnp.float32
        )
    lane = lax.broadcasted_iota(jnp.int32, (16, 256), 1)
    row16 = lax.broadcasted_iota(jnp.int32, (16, 256), 0)
    spread_out = jnp.where(lax.bitwise_and(lane, 15) == row16, 1.0, 0.0)
    placed = lax.dot_general(
        counts,
        spread_out,
        (((1,), (0,)), ((), ())),
        preferred_element_type=jnp.float32,
        precision=lax.Precision.HIGHEST,
    )
    flat = jnp.sum(jnp.where(lax.shift_right_logical(lane, 4) == row16, placed, 0.0), axis=0, keepdims=True)
    amount = jnp.broadcast_to(jnp.sum(live, axis=1, keepdims=True), (1, LANES))

    def halves(value):
        high = jnp.floor(value * (1.0 / 256.0))
        return high, value - high * 256.0

    flat_high, flat_low = halves(flat)
    rows = [flat_high[:, :LANES], flat_high[:, LANES:], flat_low[:, :LANES], flat_low[:, LANES:]]
    rows += list(halves(amount)) + [jnp.zeros((2, LANES), jnp.float32)]
    for i in range(tiles):
        fetch(i).wait()
    lane = lax.shift_right_logical(lax.broadcasted_iota(jnp.int32, tile_ref.shape[1:], 1), 3)
    energies = [tile_ref[i].astype(jnp.float32) for i in range(tiles)]
    for j in range(out_ref.shape[0]):
        piece = energies[j]
        for i in range(tiles):
            if i != j:
                piece = jnp.where(lane == i, pltpu.roll(energies[i], (8 * (i - j)) % LANES, 1), piece)
        out_ref[j] = jnp.concatenate([piece] + rows, axis=0).astype(jnp.bfloat16)


def prepare(group, anchor, energy, copies, groups):
    total = anchor.shape[0]
    components = energy.shape[0]
    return pl.pallas_call(
        prepare_kernel,
        out_shape=jax.ShapeDtypeStruct((copies, components + 8, LANES), jnp.bfloat16),
        grid_spec=pltpu.PrefetchScalarGridSpec(
            num_scalar_prefetch=1,
            grid=(1,),
            in_specs=[
                pl.BlockSpec((1, total), lambda i, g: (0, 0)),
                pl.BlockSpec(memory_space=pltpu.HBM),
            ],
            out_specs=pl.BlockSpec((copies, components + 8, LANES), lambda i, g: (0, 0, 0)),
            scratch_shapes=[
                pltpu.VMEM((groups, components, LANES), jnp.bfloat16),
                pltpu.SemaphoreType.DMA((groups,)),
            ],
        ),
        compiler_params=pltpu.CompilerParams(vmem_limit_bytes=56 * 2**20),
        name="prepare",
    )(group, anchor.reshape(1, total), energy)


def arrange_kernel(group_ref, own_ref, pieces_ref, left_ref, amount_ref, wide_ref):
    components = pieces_ref.shape[1] - 8
    wide_ref[...] = jnp.zeros_like(wide_ref)
    lane = lax.broadcasted_iota(jnp.int32, (1, LANES), 1)
    row = lax.broadcasted_iota(jnp.int32, (DEPTH - 3 * components, LANES), 0)
    at = jnp.int32(0)
    for b in range(pieces_ref.shape[0]):
        piece = pieces_ref[b].astype(jnp.float32)
        rest = piece[components:]
        is_live = live_rows(group_ref[0], own_ref[0], rest[4:5] * 256.0 + rest[5:6])
        live = jnp.where(is_live, 1.0, 0.0)
        starts = jnp.where(lax.bitwise_and(lane, 7) == 0, live, 0.0)
        energy = piece[:components] * live
        tail = jnp.where(row < SHIFT_AT - WEIGHT_AT, 1.0, jnp.where(row == LIVE_AT - WEIGHT_AT, live, 0.0))
        block = jnp.concatenate([energy, energy, energy, tail], axis=0)
        wide_ref[pl.ds(pl.multiple_of(at, 8), LANES), :] = block.T
        at = at + 8 * jnp.sum(starts).astype(jnp.int32)
    left_ref[...] = wide_ref[...].astype(jnp.bfloat16)
    amount_ref[0] = at


def arrange(group, own, pieces):
    most = pl.cdiv(pieces.shape[0] * LANES, ROW_TILE) * ROW_TILE
    smem = pl.BlockSpec(memory_space=pltpu.SMEM)
    vmem = pl.BlockSpec(memory_space=pltpu.VMEM)
    return pl.pallas_call(
        arrange_kernel,
        out_shape=[
            jax.ShapeDtypeStruct((most, DEPTH), jnp.bfloat16),
            jax.ShapeDtypeStruct((1,), jnp.int32),
        ],
        in_specs=[smem, smem, vmem],
        out_specs=[vmem, smem],
        scratch_shapes=[pltpu.VMEM((most, DEPTH), jnp.float32)],
        compiler_params=pltpu.CompilerParams(vmem_limit_bytes=6 * 2**20),
        name="arrange",
    )(group, own, pieces)


def pack_kernel(pieces_ref, start_ref, coef_ref, out_ref):
    components = coef_ref.shape[0]
    counts = jnp.sum(pieces_ref[:, components:, :].astype(jnp.float32), axis=0)
    counts = jnp.concatenate([counts[0:1], counts[1:2]], axis=1) * 256.0 + jnp.concatenate(
        [counts[2:3], counts[3:4]], axis=1
    )
    rows = list(split3(jnp.log(counts))) + list(split3(start_ref[...]))
    rows.append(jnp.zeros((2, STATE_TILE), jnp.float32))
    packed = jnp.concatenate([coef_ref[...].astype(jnp.float32)] + rows, axis=0).astype(jnp.bfloat16)
    out_ref[...] = jnp.broadcast_to(packed[None], out_ref.shape)


def pack(pieces, f_start, coef, copies):
    components, states = coef.shape
    return pl.pallas_call(
        pack_kernel,
        out_shape=jax.ShapeDtypeStruct((copies, components + 8, states), jnp.bfloat16),
        compiler_params=pltpu.CompilerParams(vmem_limit_bytes=4 * 2**20),
        name="pack",
    )(pieces, f_start.reshape(1, states), coef)


def merge_logs(parts):
    highest = jnp.max(parts, axis=0)
    return highest + jnp.log2(jnp.sum(jnp.exp2(parts - highest[None]), axis=0))


def merge_kernel(parts_ref, out_ref):
    out_ref[...] = jnp.broadcast_to(merge_logs(parts_ref[...])[None], out_ref.shape)


def merge(parts, copies):
    return pl.pallas_call(
        merge_kernel,
        out_shape=jax.ShapeDtypeStruct((copies,) + parts.shape[1:], jnp.float32),
        compiler_params=pltpu.CompilerParams(vmem_limit_bytes=4 * 2**20),
        name="merge",
    )(parts)


def centered(value):
    mean = jnp.sum(jnp.sum(value, axis=1, keepdims=True), axis=0, keepdims=True) / value.size
    return value - mean


def largest(value):
    return jnp.max(jnp.max(value, axis=1, keepdims=True), axis=0, keepdims=True)


def folded(value, combine):
    return combine(value[:, :LANES], value[:, LANES:])


def sweep_kernel(first, *refs):
    if first:
        amount_ref, packed_ref, left_ref, part_ref, wide_ref, shifted_ref, right_ref, scaled_ref, acc_ref, some_ref, tall_ref, top_ref = refs
        source_ref = shifted_ref
    else:
        amount_ref, packed_ref, left_ref, parts_ref, old_ref, part_ref, wide_ref, some_ref, right_ref, scaled_ref, acc_ref, tall_ref, top_ref = refs
        source_ref = left_ref
    groups, packed_rows, _ = packed_ref.shape
    components = packed_rows - 8
    states = groups * STATE_TILE
    pair = STATE_TILE // LANES
    amount = amount_ref[0]
    tiles = (amount + ROW_TILE - 1) // ROW_TILE

    for g in range(groups):
        rows = packed_ref[g, components:, :].astype(jnp.float32)
        log_counts = rows[0:1] + rows[1:2] + rows[2:3]
        value = log_counts + (rows[3:4] + rows[4:5] + rows[5:6]) if first else log_counts
        for h in range(pair):
            wide_ref[pair * g + h : pair * g + h + 1, :] = value[:, h * LANES : (h + 1) * LANES]
    if first:
        weights = wide_ref[...]
    else:
        raw = old_ref[...] - merge_logs(parts_ref[...]) * LN2
        wide = wide_ref[...] + centered(raw)
        wide_ref[...] = wide
        weights = wide - largest(wide - old_ref[...])
    w0, w1, w2 = split3(weights * LOG2E)

    row = lax.broadcasted_iota(jnp.int32, (DEPTH - 3 * components, LANES), 0)
    ones = jnp.where(row < LIVE_AT - WEIGHT_AT, 1.0, 0.0)
    for g in range(groups):
        coef = packed_ref[g, :components, :].astype(jnp.float32) * (-LOG2E)
        lanes = slice(g * STATE_TILE, (g + 1) * STATE_TILE)
        for k, part in enumerate(split3(coef)):
            right_ref[k * components : (k + 1) * components, lanes] = part.astype(jnp.bfloat16)
        for h in range(pair):
            at = pair * g + h
            tail = jnp.where(row == 0, w0[at : at + 1], jnp.where(row == 1, w1[at : at + 1], jnp.where(row == 2, w2[at : at + 1], ones)))
            right_ref[WEIGHT_AT:, at * LANES : (at + 1) * LANES] = tail.astype(jnp.bfloat16)

    def product(left, right):
        return lax.dot_general(left, right, (((1,), (0,)), ((), ())), preferred_element_type=jnp.float32)

    if first:
        lane = lax.broadcasted_iota(jnp.int32, (DEPTH, LANES), 1)
        for h in range(2):
            some = jnp.zeros((DEPTH, LANES), jnp.float32)
            for j in range(8):
                g = 8 * h + j
                tile = right_ref[:, g * STATE_TILE : g * STATE_TILE + LANES].astype(jnp.float32)
                moved = tile if j == 0 else pltpu.roll(tile, 16 * j, 1)
                some = jnp.where(lax.shift_right_logical(lane, 4) == j, moved, some)
            some_ref[:, h * LANES : (h + 1) * LANES] = some.astype(jnp.bfloat16)

    acc_ref[...] = jnp.zeros_like(acc_ref)
    lane = lax.broadcasted_iota(jnp.int32, (ROW_TILE, LANES), 1)

    def shifted(block, shift):
        s0, s1, s2 = split3(-shift)
        values = jnp.where(lane == SHIFT_AT, s0, jnp.where(lane == SHIFT_AT + 1, s1, s2))
        chosen = jnp.logical_and(lane >= SHIFT_AT, lane < LIVE_AT)
        return jnp.where(chosen, values, block.astype(jnp.float32)).astype(jnp.bfloat16)

    def visit(t, carry):
        least, most = carry
        rows = pl.ds(pl.multiple_of(t * ROW_TILE, ROW_TILE), ROW_TILE)
        left = left_ref[rows, :]
        if first:
            sampled = folded(product(left, some_ref[...]), jnp.maximum)
            shift = jnp.max(sampled, axis=1, keepdims=True)
            left = shifted(left, shift)
        live = left_ref[rows, LIVE_AT : LIVE_AT + 1].astype(jnp.float32)
        total = jnp.zeros((ROW_TILE, LANES), jnp.float32)
        for g in range(groups):
            lanes = slice(g * STATE_TILE, (g + 1) * STATE_TILE)
            scaled = jnp.exp2(product(left, right_ref[:, lanes]))
            scaled_ref[:, lanes] = scaled
            total += folded(scaled, jnp.add)
        denominator = jnp.sum(total, axis=1, keepdims=True)
        least = jnp.minimum(least, jnp.where(live > 0.0, denominator, 1.0))
        most = jnp.maximum(most, jnp.where(live > 0.0, denominator, 1.0))
        share = jnp.broadcast_to(live / denominator, (ROW_TILE, LANES))
        if first:
            shifted_ref[rows, :] = shifted(left, shift + jnp.log2(denominator))
        for k in range(states // LANES):
            lanes = slice(k * LANES, (k + 1) * LANES)
            part = scaled_ref[:, lanes] * share
            acc_ref[:, lanes] += jnp.sum(part.reshape(ROW_TILE // 8, 8, LANES), axis=0)
        return least, most

    unit = jnp.ones((ROW_TILE, 1), jnp.float32)
    least, most = lax.fori_loop(0, tiles, visit, (unit, unit))
    least = jnp.min(least, axis=0, keepdims=True)
    most = jnp.max(most, axis=0, keepdims=True)
    sums = jnp.sum(acc_ref[...], axis=0, keepdims=True)
    smallest = jnp.min(sums, axis=1, keepdims=True)
    logs = jnp.where(sums > 0.0, jnp.log2(jnp.maximum(sums, SAFE_SUM)), LOW)

    def give(value):
        for k in range(states // LANES):
            tall_ref[k : k + 1, :] = value[:, k * LANES : (k + 1) * LANES]
        part_ref[...] = jnp.broadcast_to(tall_ref[...][None], part_ref.shape)

    give(logs)
    enough = jnp.logical_and(smallest >= SAFE_SUM, smallest * least >= SAFE_SUM)
    safe = jnp.logical_and(enough, jnp.logical_and(most < SAFE_TOP, least > SAFE_SUM))
    unsafe = jnp.max(jnp.where(safe, 0.0, 1.0)) > 0.0

    @pl.when(jnp.logical_and(amount > 0, unsafe))
    def exact():
        acc_ref[...] = jnp.zeros_like(acc_ref)
        top_ref[...] = jnp.full_like(top_ref, LOW)

        def tile_at(k):
            return pl.ds(pl.multiple_of(k * LANES, LANES), LANES)

        def slots(t, carry):
            rows = pl.ds(pl.multiple_of(t * ROW_TILE, ROW_TILE), ROW_TILE)
            left = left_ref[rows, :]
            is_live = jnp.broadcast_to(left[:, LIVE_AT : LIVE_AT + 1].astype(jnp.float32), (ROW_TILE, LANES)) > 0.0

            def column(k, pieces):
                high, total = pieces
                score = product(left, right_ref[:, tile_at(k)])
                newer = jnp.maximum(high, score)
                return newer, total * jnp.exp2(high - newer) + jnp.exp2(score - newer)

            start = (jnp.full((ROW_TILE, LANES), LOW, jnp.float32), jnp.zeros((ROW_TILE, LANES), jnp.float32))
            high, total = lax.fori_loop(0, states // LANES, column, start)
            top = jnp.max(high, axis=1, keepdims=True)
            total = jnp.sum(total * jnp.exp2(high - top), axis=1, keepdims=True)
            norm = top + jnp.log2(total)
            if first:
                shifted_ref[rows, :] = shifted(left, norm)

            def state(k, inner):
                lanes = tile_at(k)
                term = jnp.where(is_live, product(left, right_ref[:, lanes]) - norm, LOW)
                older = top_ref[:, lanes]
                newer = jnp.maximum(older, jnp.max(term, axis=0, keepdims=True))
                added = jnp.sum(jnp.where(is_live, jnp.exp2(term - newer), 0.0), axis=0, keepdims=True)
                acc_ref[0:1, lanes] = acc_ref[0:1, lanes] * jnp.exp2(older - newer) + added
                top_ref[:, lanes] = newer
                return inner

            return lax.fori_loop(0, states // LANES, state, carry)

        lax.fori_loop(0, tiles, slots, 0)
        give(top_ref[...] + jnp.log2(acc_ref[0:1, :]))


def sweep(amount, packed, left, parts, old, copies):
    groups = packed.shape[0]
    states = groups * STATE_TILE
    first = parts is None
    tall = states // LANES
    operands = [amount, packed, left] + ([] if first else [parts, old])
    outs = [((copies, tall, LANES), jnp.float32), ((tall, LANES), jnp.float32)]
    scratch = [
        pltpu.VMEM((DEPTH, states), jnp.bfloat16),
        pltpu.VMEM((ROW_TILE, states), jnp.float32),
        pltpu.VMEM((8, states), jnp.float32),
        pltpu.VMEM((DEPTH, 2 * LANES), jnp.bfloat16),
        pltpu.VMEM((tall, LANES), jnp.float32),
        pltpu.VMEM((1, states), jnp.float32),
    ]
    if first:
        outs.append((left.shape, jnp.bfloat16))
    else:
        scratch = [scratch[3]] + scratch[:3] + scratch[4:]
    return pl.pallas_call(
        functools.partial(sweep_kernel, first),
        out_shape=[jax.ShapeDtypeStruct(*out) for out in outs],
        in_specs=[pl.BlockSpec(memory_space=pltpu.SMEM)] + [pl.BlockSpec(memory_space=pltpu.VMEM)] * (len(operands) - 1),
        scratch_shapes=scratch,
        compiler_params=pltpu.CompilerParams(vmem_limit_bytes=20 * 2**20),
        name="first_sweep" if first else "next_sweep",
    )(*operands)


def finish_kernel(group_ref, parts_ref, old_ref, out_ref, hold_ref):
    raw = old_ref[...] - merge_logs(parts_ref[...]) * LN2
    hold_ref[...] = centered(raw)
    out_ref[...] = hold_ref[pl.ds(group_ref[0] * out_ref.shape[0], out_ref.shape[0]), :]


def finish(group, parts, old):
    rows = old.shape[0] // parts.shape[0]
    return pl.pallas_call(
        finish_kernel,
        out_shape=jax.ShapeDtypeStruct((rows, LANES), jnp.float32),
        grid_spec=pltpu.PrefetchScalarGridSpec(
            num_scalar_prefetch=1,
            grid=(1,),
            in_specs=[
                pl.BlockSpec(parts.shape, lambda i, g: (0, 0, 0)),
                pl.BlockSpec(old.shape, lambda i, g: (0, 0)),
            ],
            out_specs=pl.BlockSpec((rows, LANES), lambda i, g: (0, 0)),
            scratch_shapes=[pltpu.VMEM(old.shape, jnp.float32)],
        ),
        compiler_params=pltpu.CompilerParams(vmem_limit_bytes=4 * 2**20),
        name="finish",
    )(group, parts, old)


def spread(copies, axis):
    return lax.all_to_all(copies, axis, 0, 0)


def per_device(energy, coef, anchor, f_start):
    groups = lax.axis_size("state")
    blocks = lax.axis_size("sample")
    group = lax.axis_index("state").astype(jnp.int32).reshape(1)
    own = lax.axis_index("sample").astype(jnp.int32).reshape(1)
    pieces = spread(prepare(group, anchor, energy, blocks, groups), "sample")
    packed = spread(pack(pieces, f_start, coef, groups), "state")
    left, amount = arrange(group, own, pieces)
    parts = None
    weights = None
    for iteration in range(ITERS):
        part, weights, *rest = sweep(amount, packed, left, parts, weights, blocks)
        if rest:
            left = rest[0]
        parts = spread(merge(spread(part, "sample"), groups), "state")
    return finish(group, parts, weights).reshape(-1)


def solution(mesh):
    in_specs = (P(None, "sample"), P(None, "state"), P("sample"), P("state"))
    out_specs = P("state")
    return jax.shard_map(
        per_device, mesh=mesh, in_specs=in_specs, out_specs=out_specs, check_vma=False
    )
```

```python
import functools

import jax
import jax.numpy as jnp
from jax import lax
from jax.experimental import pallas as pl
from jax.experimental.pallas import tpu as pltpu
from jax.sharding import PartitionSpec as P

ITERS = 2

LOG2E = 1.4426950408889634
LN2 = 0.6931471805599453
LOW = -1.0e30
SAFE_SUM = 1.0e-25
SAFE_TOP = 1.0e30

LANES = 128
STATE_TILE = 256
ROW_TILE = 416
DEPTH = 128
WEIGHT_AT = 96
SHIFT_AT = 99
LIVE_AT = 102


def split3(value):
    high = value.astype(jnp.bfloat16).astype(jnp.float32)
    rest = value - high
    middle = rest.astype(jnp.bfloat16).astype(jnp.float32)
    low = (rest - middle).astype(jnp.bfloat16).astype(jnp.float32)
    return high, middle, low


def live_rows(group, own, live_slots):
    lane = lax.broadcasted_iota(jnp.int32, (1, LANES), 1)
    tile = group + 16 * lax.shift_right_logical(lane, 3)
    slot = tile * LANES + 8 * own + lax.bitwise_and(lane, 7)
    return slot.astype(jnp.float32) < live_slots


def prepare_kernel(group_ref, anchor_ref, energy_ref, out_ref, tile_ref, sems):
    group = group_ref[0]
    tiles = tile_ref.shape[0]
    tall = tiles * STATE_TILE // LANES

    def fetch(i):
        at = pl.multiple_of((group + tiles * i) * LANES, LANES)
        return pltpu.make_async_copy(energy_ref.at[:, pl.ds(at, LANES)], tile_ref.at[i], sems.at[i])

    for i in range(tiles):
        fetch(i).start()
    total = anchor_ref.shape[1]
    step = 2048
    tall_row = lax.broadcasted_iota(jnp.int32, (tall, step), 0)
    lane_row = lax.broadcasted_iota(jnp.int32, (LANES, step), 0)
    counts = jnp.zeros((tall, LANES), jnp.float32)
    for start in range(0, total, step):
        anchor = anchor_ref[:, start : start + step]
        high = lax.shift_right_logical(anchor, 7)
        low = lax.bitwise_and(anchor, LANES - 1)
        high_hot = jnp.where(tall_row == high, 1.0, 0.0).astype(jnp.bfloat16)
        low_hot = jnp.where(lane_row == low, 1.0, 0.0).astype(jnp.bfloat16)
        counts += lax.dot_general(
            high_hot, low_hot, (((1,), (1,)), ((), ())), preferred_element_type=jnp.float32
        )
    amount = jnp.sum(jnp.sum(counts, axis=1, keepdims=True), axis=0, keepdims=True)

    def halves(value):
        high = jnp.floor(value * (1.0 / 256.0))
        return [high, value - high * 256.0]

    rows = halves(counts) + halves(jnp.broadcast_to(amount, (1, LANES))) + [jnp.zeros((6, LANES), jnp.float32)]
    for i in range(tiles):
        fetch(i).wait()
    lane = lax.shift_right_logical(lax.broadcasted_iota(jnp.int32, tile_ref.shape[1:], 1), 3)
    energies = [tile_ref[i].astype(jnp.float32) for i in range(tiles)]
    for j in range(out_ref.shape[0]):
        piece = energies[j]
        for i in range(tiles):
            if i != j:
                piece = jnp.where(lane == i, pltpu.roll(energies[i], (8 * (i - j)) % LANES, 1), piece)
        out_ref[j] = jnp.concatenate([piece] + rows, axis=0).astype(jnp.bfloat16)


def prepare(group, anchor, energy, copies, groups):
    total = anchor.shape[0]
    components = energy.shape[0]
    rows = components + 2 * groups * STATE_TILE // LANES + 8
    return pl.pallas_call(
        prepare_kernel,
        out_shape=jax.ShapeDtypeStruct((copies, rows, LANES), jnp.bfloat16),
        grid_spec=pltpu.PrefetchScalarGridSpec(
            num_scalar_prefetch=1,
            grid=(1,),
            in_specs=[
                pl.BlockSpec((1, total), lambda i, g: (0, 0)),
                pl.BlockSpec(memory_space=pltpu.HBM),
            ],
            out_specs=pl.BlockSpec((copies, rows, LANES), lambda i, g: (0, 0, 0)),
            scratch_shapes=[
                pltpu.VMEM((groups, components, LANES), jnp.bfloat16),
                pltpu.SemaphoreType.DMA((groups,)),
            ],
        ),
        compiler_params=pltpu.CompilerParams(vmem_limit_bytes=56 * 2**20),
        name="prepare",
    )(group, anchor.reshape(1, total), energy)


def arrange_kernel(components, group_ref, own_ref, pieces_ref, left_ref, amount_ref, log_ref, wide_ref):
    tall = log_ref.shape[0]
    wide_ref[...] = jnp.zeros_like(wide_ref)
    lane = lax.broadcasted_iota(jnp.int32, (1, LANES), 1)
    row = lax.broadcasted_iota(jnp.int32, (DEPTH - 3 * components, LANES), 0)
    counts = jnp.zeros((tall, LANES), jnp.float32)
    at = jnp.int32(0)
    for b in range(pieces_ref.shape[0]):
        piece = pieces_ref[b].astype(jnp.float32)
        rest = piece[components:]
        counts += rest[:tall] * 256.0 + rest[tall : 2 * tall]
        is_live = live_rows(group_ref[0], own_ref[0], rest[2 * tall : 2 * tall + 1] * 256.0 + rest[2 * tall + 1 : 2 * tall + 2])
        live = jnp.where(is_live, 1.0, 0.0)
        starts = jnp.where(lax.bitwise_and(lane, 7) == 0, live, 0.0)
        energy = piece[:components] * live
        tail = jnp.where(row < SHIFT_AT - WEIGHT_AT, 1.0, jnp.where(row == LIVE_AT - WEIGHT_AT, live, 0.0))
        block = jnp.concatenate([energy, energy, energy, tail], axis=0)
        wide_ref[pl.ds(pl.multiple_of(at, 8), LANES), :] = block.T
        at = at + 8 * jnp.sum(starts).astype(jnp.int32)
    left_ref[...] = wide_ref[...].astype(jnp.bfloat16)
    amount_ref[0] = at
    log_ref[...] = jnp.log(counts)


def arrange(group, own, pieces, components, groups):
    most = pl.cdiv(pieces.shape[0] * LANES, ROW_TILE) * ROW_TILE
    smem = pl.BlockSpec(memory_space=pltpu.SMEM)
    vmem = pl.BlockSpec(memory_space=pltpu.VMEM)
    return pl.pallas_call(
        functools.partial(arrange_kernel, components),
        out_shape=[
            jax.ShapeDtypeStruct((most, DEPTH), jnp.bfloat16),
            jax.ShapeDtypeStruct((1,), jnp.int32),
            jax.ShapeDtypeStruct((groups * STATE_TILE // LANES, LANES), jnp.float32),
        ],
        in_specs=[smem, smem, vmem],
        out_specs=[vmem, smem, vmem],
        scratch_shapes=[pltpu.VMEM((most, DEPTH), jnp.float32)],
        compiler_params=pltpu.CompilerParams(vmem_limit_bytes=6 * 2**20),
        name="arrange",
    )(group, own, pieces)


def pack_kernel(start_ref, coef_ref, out_ref):
    rows = list(split3(start_ref[...])) + [jnp.zeros((5, STATE_TILE), jnp.float32)]
    packed = jnp.concatenate([coef_ref[...].astype(jnp.float32)] + rows, axis=0).astype(jnp.bfloat16)
    out_ref[...] = jnp.broadcast_to(packed[None], out_ref.shape)


def pack(f_start, coef, copies):
    components, states = coef.shape
    return pl.pallas_call(
        pack_kernel,
        out_shape=jax.ShapeDtypeStruct((copies, components + 8, states), jnp.bfloat16),
        compiler_params=pltpu.CompilerParams(vmem_limit_bytes=4 * 2**20),
        name="pack",
    )(f_start.reshape(1, states), coef)


def merge_logs(parts):
    highest = jnp.max(parts, axis=0)
    return highest + jnp.log2(jnp.sum(jnp.exp2(parts - highest[None]), axis=0))


def merge_kernel(parts_ref, out_ref):
    out_ref[...] = jnp.broadcast_to(merge_logs(parts_ref[...])[None], out_ref.shape)


def merge(parts, copies):
    return pl.pallas_call(
        merge_kernel,
        out_shape=jax.ShapeDtypeStruct((copies,) + parts.shape[1:], jnp.float32),
        compiler_params=pltpu.CompilerParams(vmem_limit_bytes=4 * 2**20),
        name="merge",
    )(parts)


def centered(value):
    mean = jnp.sum(jnp.sum(value, axis=1, keepdims=True), axis=0, keepdims=True) / value.size
    return value - mean


def largest(value):
    return jnp.max(jnp.max(value, axis=1, keepdims=True), axis=0, keepdims=True)


def folded(value, combine):
    return combine(value[:, :LANES], value[:, LANES:])


def sweep_kernel(first, *refs):
    if first:
        amount_ref, packed_ref, log_ref, left_ref, part_ref, wide_ref, shifted_ref, right_ref, scaled_ref, acc_ref, some_ref, tall_ref, top_ref = refs
        source_ref = shifted_ref
    else:
        amount_ref, packed_ref, log_ref, left_ref, parts_ref, old_ref, part_ref, wide_ref, some_ref, right_ref, scaled_ref, acc_ref, tall_ref, top_ref = refs
        source_ref = left_ref
    groups, packed_rows, _ = packed_ref.shape
    components = packed_rows - 8
    states = groups * STATE_TILE
    pair = STATE_TILE // LANES
    amount = amount_ref[0]
    tiles = (amount + ROW_TILE - 1) // ROW_TILE

    if first:
        for g in range(groups):
            rows = packed_ref[g, components : components + 3, :].astype(jnp.float32)
            start = rows[0:1] + rows[1:2] + rows[2:3]
            for h in range(pair):
                wide_ref[pair * g + h : pair * g + h + 1, :] = start[:, h * LANES : (h + 1) * LANES]
        weights = wide_ref[...] + log_ref[...]
        wide_ref[...] = weights
    else:
        raw = old_ref[...] - merge_logs(parts_ref[...]) * LN2
        wide = log_ref[...] + centered(raw)
        wide_ref[...] = wide
        weights = wide - largest(wide - old_ref[...])
    w0, w1, w2 = split3(weights * LOG2E)

    row = lax.broadcasted_iota(jnp.int32, (DEPTH - 3 * components, LANES), 0)
    ones = jnp.where(row < LIVE_AT - WEIGHT_AT, 1.0, 0.0)
    for g in range(groups):
        coef = packed_ref[g, :components, :].astype(jnp.float32) * (-LOG2E)
        lanes = slice(g * STATE_TILE, (g + 1) * STATE_TILE)
        for k, part in enumerate(split3(coef)):
            right_ref[k * components : (k + 1) * components, lanes] = part.astype(jnp.bfloat16)
        for h in range(pair):
            at = pair * g + h
            tail = jnp.where(row == 0, w0[at : at + 1], jnp.where(row == 1, w1[at : at + 1], jnp.where(row == 2, w2[at : at + 1], ones)))
            right_ref[WEIGHT_AT:, at * LANES : (at + 1) * LANES] = tail.astype(jnp.bfloat16)

    def product(left, right):
        return lax.dot_general(left, right, (((1,), (0,)), ((), ())), preferred_element_type=jnp.float32)

    if first:
        lane = lax.broadcasted_iota(jnp.int32, (DEPTH, LANES), 1)
        for h in range(2):
            some = jnp.zeros((DEPTH, LANES), jnp.float32)
            for j in range(8):
                g = 8 * h + j
                tile = right_ref[:, g * STATE_TILE : g * STATE_TILE + LANES].astype(jnp.float32)
                moved = tile if j == 0 else pltpu.roll(tile, 16 * j, 1)
                some = jnp.where(lax.shift_right_logical(lane, 4) == j, moved, some)
            some_ref[:, h * LANES : (h + 1) * LANES] = some.astype(jnp.bfloat16)

    acc_ref[...] = jnp.zeros_like(acc_ref)
    lane = lax.broadcasted_iota(jnp.int32, (ROW_TILE, LANES), 1)

    def shifted(block, shift):
        s0, s1, s2 = split3(-shift)
        values = jnp.where(lane == SHIFT_AT, s0, jnp.where(lane == SHIFT_AT + 1, s1, s2))
        chosen = jnp.logical_and(lane >= SHIFT_AT, lane < LIVE_AT)
        return jnp.where(chosen, values, block.astype(jnp.float32)).astype(jnp.bfloat16)

    def visit(t, carry):
        least, most = carry
        rows = pl.ds(pl.multiple_of(t * ROW_TILE, ROW_TILE), ROW_TILE)
        left = left_ref[rows, :]
        if first:
            sampled = folded(product(left, some_ref[...]), jnp.maximum)
            shift = jnp.max(sampled, axis=1, keepdims=True)
            left = shifted(left, shift)
        live = left_ref[rows, LIVE_AT : LIVE_AT + 1].astype(jnp.float32)
        total = jnp.zeros((ROW_TILE, LANES), jnp.float32)
        for g in range(groups):
            lanes = slice(g * STATE_TILE, (g + 1) * STATE_TILE)
            scaled = jnp.exp2(product(left, right_ref[:, lanes]))
            scaled_ref[:, lanes] = scaled
            total += folded(scaled, jnp.add)
        denominator = jnp.sum(total, axis=1, keepdims=True)
        least = jnp.minimum(least, jnp.where(live > 0.0, denominator, 1.0))
        most = jnp.maximum(most, jnp.where(live > 0.0, denominator, 1.0))
        share = jnp.broadcast_to(live / denominator, (ROW_TILE, LANES))
        if first:
            shifted_ref[rows, :] = shifted(left, shift + jnp.log2(denominator))
        for k in range(states // LANES):
            lanes = slice(k * LANES, (k + 1) * LANES)
            part = scaled_ref[:, lanes] * share
            acc_ref[:, lanes] += jnp.sum(part.reshape(ROW_TILE // 8, 8, LANES), axis=0)
        return least, most

    unit = jnp.ones((ROW_TILE, 1), jnp.float32)
    least, most = lax.fori_loop(0, tiles, visit, (unit, unit))
    least = jnp.min(least, axis=0, keepdims=True)
    most = jnp.max(most, axis=0, keepdims=True)
    sums = jnp.sum(acc_ref[...], axis=0, keepdims=True)
    smallest = jnp.min(sums, axis=1, keepdims=True)
    logs = jnp.where(sums > 0.0, jnp.log2(jnp.maximum(sums, SAFE_SUM)), LOW)

    def give(value):
        for k in range(states // LANES):
            tall_ref[k : k + 1, :] = value[:, k * LANES : (k + 1) * LANES]
        part_ref[...] = jnp.broadcast_to(tall_ref[...][None], part_ref.shape)

    give(logs)
    enough = jnp.logical_and(smallest >= SAFE_SUM, smallest * least >= SAFE_SUM)
    safe = jnp.logical_and(enough, jnp.logical_and(most < SAFE_TOP, least > SAFE_SUM))
    unsafe = jnp.max(jnp.where(safe, 0.0, 1.0)) > 0.0

    @pl.when(jnp.logical_and(amount > 0, unsafe))
    def exact():
        acc_ref[...] = jnp.zeros_like(acc_ref)
        top_ref[...] = jnp.full_like(top_ref, LOW)

        def tile_at(k):
            return pl.ds(pl.multiple_of(k * LANES, LANES), LANES)

        def slots(t, carry):
            rows = pl.ds(pl.multiple_of(t * ROW_TILE, ROW_TILE), ROW_TILE)
            left = left_ref[rows, :]
            is_live = jnp.broadcast_to(left[:, LIVE_AT : LIVE_AT + 1].astype(jnp.float32), (ROW_TILE, LANES)) > 0.0

            def column(k, pieces):
                high, total = pieces
                score = product(left, right_ref[:, tile_at(k)])
                newer = jnp.maximum(high, score)
                return newer, total * jnp.exp2(high - newer) + jnp.exp2(score - newer)

            start = (jnp.full((ROW_TILE, LANES), LOW, jnp.float32), jnp.zeros((ROW_TILE, LANES), jnp.float32))
            high, total = lax.fori_loop(0, states // LANES, column, start)
            top = jnp.max(high, axis=1, keepdims=True)
            total = jnp.sum(total * jnp.exp2(high - top), axis=1, keepdims=True)
            norm = top + jnp.log2(total)
            if first:
                shifted_ref[rows, :] = shifted(left, norm)

            def state(k, inner):
                lanes = tile_at(k)
                term = jnp.where(is_live, product(left, right_ref[:, lanes]) - norm, LOW)
                older = top_ref[:, lanes]
                newer = jnp.maximum(older, jnp.max(term, axis=0, keepdims=True))
                added = jnp.sum(jnp.where(is_live, jnp.exp2(term - newer), 0.0), axis=0, keepdims=True)
                acc_ref[0:1, lanes] = acc_ref[0:1, lanes] * jnp.exp2(older - newer) + added
                top_ref[:, lanes] = newer
                return inner

            return lax.fori_loop(0, states // LANES, state, carry)

        lax.fori_loop(0, tiles, slots, 0)
        give(top_ref[...] + jnp.log2(acc_ref[0:1, :]))


def sweep(amount, packed, log_counts, left, parts, old, copies):
    groups = packed.shape[0]
    states = groups * STATE_TILE
    first = parts is None
    tall = states // LANES
    operands = [amount, packed, log_counts, left] + ([] if first else [parts, old])
    outs = [((copies, tall, LANES), jnp.float32), ((tall, LANES), jnp.float32)]
    scratch = [
        pltpu.VMEM((DEPTH, states), jnp.bfloat16),
        pltpu.VMEM((ROW_TILE, states), jnp.float32),
        pltpu.VMEM((8, states), jnp.float32),
        pltpu.VMEM((DEPTH, 2 * LANES), jnp.bfloat16),
        pltpu.VMEM((tall, LANES), jnp.float32),
        pltpu.VMEM((1, states), jnp.float32),
    ]
    if first:
        outs.append((left.shape, jnp.bfloat16))
    else:
        scratch = [scratch[3]] + scratch[:3] + scratch[4:]
    return pl.pallas_call(
        functools.partial(sweep_kernel, first),
        out_shape=[jax.ShapeDtypeStruct(*out) for out in outs],
        in_specs=[pl.BlockSpec(memory_space=pltpu.SMEM)] + [pl.BlockSpec(memory_space=pltpu.VMEM)] * (len(operands) - 1),
        scratch_shapes=scratch,
        compiler_params=pltpu.CompilerParams(vmem_limit_bytes=20 * 2**20),
        name="first_sweep" if first else "next_sweep",
    )(*operands)


def finish_kernel(group_ref, parts_ref, old_ref, out_ref, hold_ref):
    raw = old_ref[...] - merge_logs(parts_ref[...]) * LN2
    hold_ref[...] = centered(raw)
    out_ref[...] = hold_ref[pl.ds(group_ref[0] * out_ref.shape[0], out_ref.shape[0]), :]


def finish(group, parts, old):
    rows = old.shape[0] // parts.shape[0]
    return pl.pallas_call(
        finish_kernel,
        out_shape=jax.ShapeDtypeStruct((rows, LANES), jnp.float32),
        grid_spec=pltpu.PrefetchScalarGridSpec(
            num_scalar_prefetch=1,
            grid=(1,),
            in_specs=[
                pl.BlockSpec(parts.shape, lambda i, g: (0, 0, 0)),
                pl.BlockSpec(old.shape, lambda i, g: (0, 0)),
            ],
            out_specs=pl.BlockSpec((rows, LANES), lambda i, g: (0, 0)),
            scratch_shapes=[pltpu.VMEM(old.shape, jnp.float32)],
        ),
        compiler_params=pltpu.CompilerParams(vmem_limit_bytes=4 * 2**20),
        name="finish",
    )(group, parts, old)


def spread(copies, axis):
    return lax.all_to_all(copies, axis, 0, 0)


def per_device(energy, coef, anchor, f_start):
    groups = lax.axis_size("state")
    blocks = lax.axis_size("sample")
    group = lax.axis_index("state").astype(jnp.int32).reshape(1)
    own = lax.axis_index("sample").astype(jnp.int32).reshape(1)
    packed = spread(pack(f_start, coef, groups), "state")
    prepared = prepare(group, anchor, energy, blocks, groups)
    prepared, packed = lax.optimization_barrier((prepared, packed))
    pieces = spread(prepared, "sample")
    left, amount, log_counts = arrange(group, own, pieces, energy.shape[0], groups)
    parts = None
    weights = None
    for iteration in range(ITERS):
        part, weights, *rest = sweep(amount, packed, log_counts, left, parts, weights, blocks)
        if rest:
            left = rest[0]
        parts = spread(merge(spread(part, "sample"), groups), "state")
    return finish(group, parts, weights).reshape(-1)


def solution(mesh):
    in_specs = (P(None, "sample"), P(None, "state"), P("sample"), P("state"))
    out_specs = P("state")
    return jax.shard_map(
        per_device, mesh=mesh, in_specs=in_specs, out_specs=out_specs, check_vma=False
    )
```

```python
import functools

import jax
import jax.numpy as jnp
from jax import lax
from jax.experimental import pallas as pl
from jax.experimental.pallas import tpu as pltpu
from jax.sharding import PartitionSpec as P

ITERS = 2

LOG2E = 1.4426950408889634
LN2 = 0.6931471805599453
LOW = -1.0e30
SAFE_SUM = 1.0e-25
SAFE_TOP = 1.0e30

LANES = 128
STATE_TILE = 256
ROW_TILE = 416
DEPTH = 128
WEIGHT_AT = 96
SHIFT_AT = 99
LIVE_AT = 102


def split3(value):
    high = value.astype(jnp.bfloat16).astype(jnp.float32)
    rest = value - high
    middle = rest.astype(jnp.bfloat16).astype(jnp.float32)
    low = (rest - middle).astype(jnp.bfloat16).astype(jnp.float32)
    return high, middle, low


def live_rows(group, own, live_slots):
    lane = lax.broadcasted_iota(jnp.int32, (1, LANES), 1)
    tile = group + 16 * lax.shift_right_logical(lane, 3)
    slot = tile * LANES + 8 * own + lax.bitwise_and(lane, 7)
    return slot.astype(jnp.float32) < live_slots


def prepare_kernel(group_ref, anchor_ref, energy_ref, out_ref, tile_ref, sems):
    group = group_ref[0]
    tiles = tile_ref.shape[0]

    def fetch(i):
        at = pl.multiple_of((group + tiles * i) * LANES, LANES)
        return pltpu.make_async_copy(energy_ref.at[:, pl.ds(at, LANES)], tile_ref.at[i], sems.at[i])

    for i in range(tiles):
        fetch(i).start()
    base = group * 16
    total = anchor_ref.shape[1]
    step = 4096
    row = lax.broadcasted_iota(jnp.int32, (16, step), 0)
    counts = jnp.zeros((16, 16), jnp.float32)
    live = jnp.zeros((1, step), jnp.float32)
    for start in range(0, total, step):
        anchor = anchor_ref[:, start : start + step]
        high = lax.shift_right_logical(anchor, 4) - base
        low = lax.bitwise_and(anchor, 15)
        high_hot = jnp.where(row == high, 1.0, 0.0).astype(jnp.bfloat16)
        low_hot = jnp.where(row == low, 1.0, 0.0).astype(jnp.bfloat16)
        live += jnp.where(anchor < tiles * STATE_TILE, 1.0, 0.0)
        counts += lax.dot_general(
            high_hot, low_hot, (((1,), (1,)), ((), ())), preferred_element_type=jnp.float32
        )
    lane = lax.broadcasted_iota(jnp.int32, (16, 256), 1)
    row16 = lax.broadcasted_iota(jnp.int32, (16, 256), 0)
    spread_out = jnp.where(lax.bitwise_and(lane, 15) == row16, 1.0, 0.0)
    placed = lax.dot_general(
        counts,
        spread_out,
        (((1,), (0,)), ((), ())),
        preferred_element_type=jnp.float32,
        precision=lax.Precision.HIGHEST,
    )
    flat = jnp.sum(jnp.where(lax.shift_right_logical(lane, 4) == row16, placed, 0.0), axis=0, keepdims=True)
    amount = jnp.broadcast_to(jnp.sum(live, axis=1, keepdims=True), (1, LANES))

    def halves(value):
        high = jnp.floor(value * (1.0 / 256.0))
        return high, value - high * 256.0

    flat_high, flat_low = halves(flat)
    rows = [flat_high[:, :LANES], flat_high[:, LANES:], flat_low[:, :LANES], flat_low[:, LANES:]]
    rows += list(halves(amount)) + [jnp.zeros((2, LANES), jnp.float32)]
    for i in range(tiles):
        fetch(i).wait()
    lane = lax.shift_right_logical(lax.broadcasted_iota(jnp.int32, tile_ref.shape[1:], 1), 3)
    energies = [tile_ref[i].astype(jnp.float32) for i in range(tiles)]
    for j in range(out_ref.shape[0]):
        piece = energies[j]
        for i in range(tiles):
            if i != j:
                piece = jnp.where(lane == i, pltpu.roll(energies[i], (8 * (i - j)) % LANES, 1), piece)
        out_ref[j] = jnp.concatenate([piece] + rows, axis=0).astype(jnp.bfloat16)


def prepare(group, anchor, energy, copies, groups):
    total = anchor.shape[0]
    components = energy.shape[0]
    return pl.pallas_call(
        prepare_kernel,
        out_shape=jax.ShapeDtypeStruct((copies, components + 8, LANES), jnp.bfloat16),
        grid_spec=pltpu.PrefetchScalarGridSpec(
            num_scalar_prefetch=1,
            grid=(1,),
            in_specs=[
                pl.BlockSpec((1, total), lambda i, g: (0, 0)),
                pl.BlockSpec(memory_space=pltpu.HBM),
            ],
            out_specs=pl.BlockSpec((copies, components + 8, LANES), lambda i, g: (0, 0, 0)),
            scratch_shapes=[
                pltpu.VMEM((groups, components, LANES), jnp.bfloat16),
                pltpu.SemaphoreType.DMA((groups,)),
            ],
        ),
        compiler_params=pltpu.CompilerParams(vmem_limit_bytes=56 * 2**20),
        name="prepare",
    )(group, anchor.reshape(1, total), energy)


def arrange_kernel(group_ref, own_ref, pieces_ref, left_ref, amount_ref, wide_ref):
    components = pieces_ref.shape[1] - 8
    wide_ref[...] = jnp.zeros_like(wide_ref)
    lane = lax.broadcasted_iota(jnp.int32, (1, LANES), 1)
    row = lax.broadcasted_iota(jnp.int32, (DEPTH - 3 * components, LANES), 0)
    at = jnp.int32(0)
    for b in range(pieces_ref.shape[0]):
        piece = pieces_ref[b].astype(jnp.float32)
        rest = piece[components:]
        is_live = live_rows(group_ref[0], own_ref[0], rest[4:5] * 256.0 + rest[5:6])
        live = jnp.where(is_live, 1.0, 0.0)
        starts = jnp.where(lax.bitwise_and(lane, 7) == 0, live, 0.0)
        energy = piece[:components] * live
        tail = jnp.where(row < SHIFT_AT - WEIGHT_AT, 1.0, jnp.where(row == LIVE_AT - WEIGHT_AT, live, 0.0))
        block = jnp.concatenate([energy, energy, energy, tail], axis=0)
        wide_ref[pl.ds(pl.multiple_of(at, 8), LANES), :] = block.T
        at = at + 8 * jnp.sum(starts).astype(jnp.int32)
    left_ref[...] = wide_ref[...].astype(jnp.bfloat16)
    amount_ref[0] = at


def arrange(group, own, pieces):
    most = pl.cdiv(pieces.shape[0] * LANES, ROW_TILE) * ROW_TILE
    smem = pl.BlockSpec(memory_space=pltpu.SMEM)
    vmem = pl.BlockSpec(memory_space=pltpu.VMEM)
    return pl.pallas_call(
        arrange_kernel,
        out_shape=[
            jax.ShapeDtypeStruct((most, DEPTH), jnp.bfloat16),
            jax.ShapeDtypeStruct((1,), jnp.int32),
        ],
        in_specs=[smem, smem, vmem],
        out_specs=[vmem, smem],
        scratch_shapes=[pltpu.VMEM((most, DEPTH), jnp.float32)],
        compiler_params=pltpu.CompilerParams(vmem_limit_bytes=6 * 2**20),
        name="arrange",
    )(group, own, pieces)


def pack_kernel(pieces_ref, start_ref, coef_ref, out_ref):
    components = coef_ref.shape[0]
    counts = jnp.sum(pieces_ref[:, components:, :].astype(jnp.float32), axis=0)
    counts = jnp.concatenate([counts[0:1], counts[1:2]], axis=1) * 256.0 + jnp.concatenate(
        [counts[2:3], counts[3:4]], axis=1
    )
    rows = list(split3(jnp.log(counts))) + list(split3(start_ref[...]))
    rows.append(jnp.zeros((2, STATE_TILE), jnp.float32))
    packed = jnp.concatenate([coef_ref[...].astype(jnp.float32)] + rows, axis=0).astype(jnp.bfloat16)
    out_ref[...] = jnp.broadcast_to(packed[None], out_ref.shape)


def pack(pieces, f_start, coef, copies):
    components, states = coef.shape
    return pl.pallas_call(
        pack_kernel,
        out_shape=jax.ShapeDtypeStruct((copies, components + 8, states), jnp.bfloat16),
        compiler_params=pltpu.CompilerParams(vmem_limit_bytes=4 * 2**20),
        name="pack",
    )(pieces, f_start.reshape(1, states), coef)


def merge_logs(parts):
    highest = jnp.max(parts, axis=0)
    return highest + jnp.log2(jnp.sum(jnp.exp2(parts - highest[None]), axis=0))


def merge_pair_kernel(kept_ref, other_ref, out_ref):
    kept = kept_ref[...]
    other = other_ref[...]
    highest = jnp.maximum(kept, other)
    value = highest + jnp.log2(jnp.exp2(kept - highest) + jnp.exp2(other - highest))
    out_ref[...] = jnp.broadcast_to(value[None], out_ref.shape)


def merge_pair(kept, other, copies):
    return pl.pallas_call(
        merge_pair_kernel,
        out_shape=jax.ShapeDtypeStruct((copies,) + kept.shape, jnp.float32),
        compiler_params=pltpu.CompilerParams(vmem_limit_bytes=4 * 2**20),
        name="merge_pair",
    )(kept, other)


def merge_kernel(parts_ref, out_ref):
    out_ref[...] = jnp.broadcast_to(merge_logs(parts_ref[...])[None], out_ref.shape)


def merge(parts, copies):
    return pl.pallas_call(
        merge_kernel,
        out_shape=jax.ShapeDtypeStruct((copies,) + parts.shape[1:], jnp.float32),
        compiler_params=pltpu.CompilerParams(vmem_limit_bytes=4 * 2**20),
        name="merge",
    )(parts)


def centered(value):
    mean = jnp.sum(jnp.sum(value, axis=1, keepdims=True), axis=0, keepdims=True) / value.size
    return value - mean


def largest(value):
    return jnp.max(jnp.max(value, axis=1, keepdims=True), axis=0, keepdims=True)


def folded(value, combine):
    return combine(value[:, :LANES], value[:, LANES:])


def sweep_kernel(first, *refs):
    if first:
        amount_ref, own_ref, packed_ref, left_ref, kept_ref, sent_ref, wide_ref, shifted_ref, right_ref, scaled_ref, acc_ref, some_ref, tall_ref, top_ref = refs
        source_ref = shifted_ref
    else:
        amount_ref, own_ref, packed_ref, left_ref, parts_ref, old_ref, kept_ref, sent_ref, wide_ref, some_ref, right_ref, scaled_ref, acc_ref, tall_ref, top_ref = refs
        source_ref = left_ref
    groups, packed_rows, _ = packed_ref.shape
    components = packed_rows - 8
    states = groups * STATE_TILE
    pair = STATE_TILE // LANES
    amount = amount_ref[0]
    tiles = (amount + ROW_TILE - 1) // ROW_TILE

    for g in range(groups):
        rows = packed_ref[g, components:, :].astype(jnp.float32)
        log_counts = rows[0:1] + rows[1:2] + rows[2:3]
        value = log_counts + (rows[3:4] + rows[4:5] + rows[5:6]) if first else log_counts
        for h in range(pair):
            wide_ref[pair * g + h : pair * g + h + 1, :] = value[:, h * LANES : (h + 1) * LANES]
    if first:
        weights = wide_ref[...]
    else:
        raw = old_ref[...] - merge_logs(parts_ref[...]) * LN2
        wide = wide_ref[...] + centered(raw)
        wide_ref[...] = wide
        weights = wide - largest(wide - old_ref[...])
    w0, w1, w2 = split3(weights * LOG2E)

    row = lax.broadcasted_iota(jnp.int32, (DEPTH - 3 * components, LANES), 0)
    ones = jnp.where(row < LIVE_AT - WEIGHT_AT, 1.0, 0.0)
    for g in range(groups):
        coef = packed_ref[g, :components, :].astype(jnp.float32) * (-LOG2E)
        lanes = slice(g * STATE_TILE, (g + 1) * STATE_TILE)
        for k, part in enumerate(split3(coef)):
            right_ref[k * components : (k + 1) * components, lanes] = part.astype(jnp.bfloat16)
        for h in range(pair):
            at = pair * g + h
            tail = jnp.where(row == 0, w0[at : at + 1], jnp.where(row == 1, w1[at : at + 1], jnp.where(row == 2, w2[at : at + 1], ones)))
            right_ref[WEIGHT_AT:, at * LANES : (at + 1) * LANES] = tail.astype(jnp.bfloat16)

    def product(left, right):
        return lax.dot_general(left, right, (((1,), (0,)), ((), ())), preferred_element_type=jnp.float32)

    if first:
        lane = lax.broadcasted_iota(jnp.int32, (DEPTH, LANES), 1)
        for h in range(2):
            some = jnp.zeros((DEPTH, LANES), jnp.float32)
            for j in range(8):
                g = 8 * h + j
                tile = right_ref[:, g * STATE_TILE : g * STATE_TILE + LANES].astype(jnp.float32)
                moved = tile if j == 0 else pltpu.roll(tile, 16 * j, 1)
                some = jnp.where(lax.shift_right_logical(lane, 4) == j, moved, some)
            some_ref[:, h * LANES : (h + 1) * LANES] = some.astype(jnp.bfloat16)

    acc_ref[...] = jnp.zeros_like(acc_ref)
    lane = lax.broadcasted_iota(jnp.int32, (ROW_TILE, LANES), 1)

    def shifted(block, shift):
        s0, s1, s2 = split3(-shift)
        values = jnp.where(lane == SHIFT_AT, s0, jnp.where(lane == SHIFT_AT + 1, s1, s2))
        chosen = jnp.logical_and(lane >= SHIFT_AT, lane < LIVE_AT)
        return jnp.where(chosen, values, block.astype(jnp.float32)).astype(jnp.bfloat16)

    def visit(t, carry):
        least, most = carry
        rows = pl.ds(pl.multiple_of(t * ROW_TILE, ROW_TILE), ROW_TILE)
        left = left_ref[rows, :]
        if first:
            sampled = folded(product(left, some_ref[...]), jnp.maximum)
            shift = jnp.max(sampled, axis=1, keepdims=True)
            left = shifted(left, shift)
        live = left_ref[rows, LIVE_AT : LIVE_AT + 1].astype(jnp.float32)
        total = jnp.zeros((ROW_TILE, LANES), jnp.float32)
        for g in range(groups):
            lanes = slice(g * STATE_TILE, (g + 1) * STATE_TILE)
            scaled = jnp.exp2(product(left, right_ref[:, lanes]))
            scaled_ref[:, lanes] = scaled
            total += folded(scaled, jnp.add)
        denominator = jnp.sum(total, axis=1, keepdims=True)
        least = jnp.minimum(least, jnp.where(live > 0.0, denominator, 1.0))
        most = jnp.maximum(most, jnp.where(live > 0.0, denominator, 1.0))
        share = jnp.broadcast_to(live / denominator, (ROW_TILE, LANES))
        if first:
            shifted_ref[rows, :] = shifted(left, shift + jnp.log2(denominator))
        for k in range(states // LANES):
            lanes = slice(k * LANES, (k + 1) * LANES)
            part = scaled_ref[:, lanes] * share
            acc_ref[:, lanes] += jnp.sum(part.reshape(ROW_TILE // 8, 8, LANES), axis=0)
        return least, most

    unit = jnp.ones((ROW_TILE, 1), jnp.float32)
    least, most = lax.fori_loop(0, tiles, visit, (unit, unit))
    least = jnp.min(least, axis=0, keepdims=True)
    most = jnp.max(most, axis=0, keepdims=True)
    sums = jnp.sum(acc_ref[...], axis=0, keepdims=True)
    smallest = jnp.min(sums, axis=1, keepdims=True)
    logs = jnp.where(sums > 0.0, jnp.log2(jnp.maximum(sums, SAFE_SUM)), LOW)

    def give(value):
        for k in range(states // LANES):
            tall_ref[k : k + 1, :] = value[:, k * LANES : (k + 1) * LANES]
        half = kept_ref.shape[0]
        core = lax.rem(own_ref[0], 2)
        kept_ref[...] = tall_ref[pl.ds(pl.multiple_of(core * half, half), half), :]
        sent_ref[...] = tall_ref[pl.ds(pl.multiple_of((1 - core) * half, half), half), :]

    give(logs)
    enough = jnp.logical_and(smallest >= SAFE_SUM, smallest * least >= SAFE_SUM)
    safe = jnp.logical_and(enough, jnp.logical_and(most < SAFE_TOP, least > SAFE_SUM))
    unsafe = jnp.max(jnp.where(safe, 0.0, 1.0)) > 0.0

    @pl.when(jnp.logical_and(amount > 0, unsafe))
    def exact():
        acc_ref[...] = jnp.zeros_like(acc_ref)
        top_ref[...] = jnp.full_like(top_ref, LOW)

        def tile_at(k):
            return pl.ds(pl.multiple_of(k * LANES, LANES), LANES)

        def slots(t, carry):
            rows = pl.ds(pl.multiple_of(t * ROW_TILE, ROW_TILE), ROW_TILE)
            left = left_ref[rows, :]
            is_live = jnp.broadcast_to(left[:, LIVE_AT : LIVE_AT + 1].astype(jnp.float32), (ROW_TILE, LANES)) > 0.0

            def column(k, pieces):
                high, total = pieces
                score = product(left, right_ref[:, tile_at(k)])
                newer = jnp.maximum(high, score)
                return newer, total * jnp.exp2(high - newer) + jnp.exp2(score - newer)

            start = (jnp.full((ROW_TILE, LANES), LOW, jnp.float32), jnp.zeros((ROW_TILE, LANES), jnp.float32))
            high, total = lax.fori_loop(0, states // LANES, column, start)
            top = jnp.max(high, axis=1, keepdims=True)
            total = jnp.sum(total * jnp.exp2(high - top), axis=1, keepdims=True)
            norm = top + jnp.log2(total)
            if first:
                shifted_ref[rows, :] = shifted(left, norm)

            def state(k, inner):
                lanes = tile_at(k)
                term = jnp.where(is_live, product(left, right_ref[:, lanes]) - norm, LOW)
                older = top_ref[:, lanes]
                newer = jnp.maximum(older, jnp.max(term, axis=0, keepdims=True))
                added = jnp.sum(jnp.where(is_live, jnp.exp2(term - newer), 0.0), axis=0, keepdims=True)
                acc_ref[0:1, lanes] = acc_ref[0:1, lanes] * jnp.exp2(older - newer) + added
                top_ref[:, lanes] = newer
                return inner

            return lax.fori_loop(0, states // LANES, state, carry)

        lax.fori_loop(0, tiles, slots, 0)
        give(top_ref[...] + jnp.log2(acc_ref[0:1, :]))


def sweep(amount, own, packed, left, parts, old):
    groups = packed.shape[0]
    states = groups * STATE_TILE
    first = parts is None
    tall = states // LANES
    operands = [amount, own, packed, left] + ([] if first else [parts, old])
    outs = [((tall // 2, LANES), jnp.float32)] * 2 + [((tall, LANES), jnp.float32)]
    scratch = [
        pltpu.VMEM((DEPTH, states), jnp.bfloat16),
        pltpu.VMEM((ROW_TILE, states), jnp.float32),
        pltpu.VMEM((8, states), jnp.float32),
        pltpu.VMEM((DEPTH, 2 * LANES), jnp.bfloat16),
        pltpu.VMEM((tall, LANES), jnp.float32),
        pltpu.VMEM((1, states), jnp.float32),
    ]
    if first:
        outs.append((left.shape, jnp.bfloat16))
    else:
        scratch = [scratch[3]] + scratch[:3] + scratch[4:]
    return pl.pallas_call(
        functools.partial(sweep_kernel, first),
        out_shape=[jax.ShapeDtypeStruct(*out) for out in outs],
        in_specs=[pl.BlockSpec(memory_space=pltpu.SMEM)] * 2 + [pl.BlockSpec(memory_space=pltpu.VMEM)] * (len(operands) - 2),
        scratch_shapes=scratch,
        compiler_params=pltpu.CompilerParams(vmem_limit_bytes=20 * 2**20),
        name="first_sweep" if first else "next_sweep",
    )(*operands)


def finish_kernel(group_ref, parts_ref, old_ref, out_ref, hold_ref):
    raw = old_ref[...] - merge_logs(parts_ref[...]) * LN2
    hold_ref[...] = centered(raw)
    out_ref[...] = hold_ref[pl.ds(group_ref[0] * out_ref.shape[0], out_ref.shape[0]), :]


def finish(group, parts, old):
    rows = old.shape[0] // parts.shape[0]
    return pl.pallas_call(
        finish_kernel,
        out_shape=jax.ShapeDtypeStruct((rows, LANES), jnp.float32),
        grid_spec=pltpu.PrefetchScalarGridSpec(
            num_scalar_prefetch=1,
            grid=(1,),
            in_specs=[
                pl.BlockSpec(parts.shape, lambda i, g: (0, 0, 0)),
                pl.BlockSpec(old.shape, lambda i, g: (0, 0)),
            ],
            out_specs=pl.BlockSpec((rows, LANES), lambda i, g: (0, 0)),
            scratch_shapes=[pltpu.VMEM(old.shape, jnp.float32)],
        ),
        compiler_params=pltpu.CompilerParams(vmem_limit_bytes=4 * 2**20),
        name="finish",
    )(group, parts, old)


def spread(copies, axis, members=None):
    return lax.all_to_all(copies, axis, 0, 0, axis_index_groups=members)


def merged(kept, sent, groups, blocks):
    chips = blocks // 2
    other = lax.ppermute(sent, "sample", [(i, i ^ 1) for i in range(blocks)])
    lines = [[2 * z + core for z in range(chips)] for core in range(2)]
    along = spread(merge_pair(kept, other, chips), "sample", lines)
    planes = [[blocks * s + 2 * z + core for s in range(groups) for core in range(2)] for z in range(chips)]
    parts = spread(merge(along, 2 * groups), ("state", "sample"), planes)
    return parts.reshape(groups, 2 * kept.shape[0], LANES)


def per_device(energy, coef, anchor, f_start):
    groups = lax.axis_size("state")
    blocks = lax.axis_size("sample")
    group = lax.axis_index("state").astype(jnp.int32).reshape(1)
    own = lax.axis_index("sample").astype(jnp.int32).reshape(1)
    pieces = spread(prepare(group, anchor, energy, blocks, groups), "sample")
    packed = spread(pack(pieces, f_start, coef, groups), "state")
    left, amount = arrange(group, own, pieces)
    parts = None
    weights = None
    for iteration in range(ITERS):
        kept, sent, weights, *rest = sweep(amount, own, packed, left, parts, weights)
        if rest:
            left = rest[0]
        parts = merged(kept, sent, groups, blocks)
    return finish(group, parts, weights).reshape(-1)


def solution(mesh):
    in_specs = (P(None, "sample"), P(None, "state"), P("sample"), P("state"))
    out_specs = P("state")
    return jax.shard_map(
        per_device, mesh=mesh, in_specs=in_specs, out_specs=out_specs, check_vma=False
    )
```

```python
import functools

import jax
import jax.numpy as jnp
from jax import lax
from jax.experimental import pallas as pl
from jax.experimental.pallas import tpu as pltpu
from jax.sharding import PartitionSpec as P

ITERS = 2

LOG2E = 1.4426950408889634
LN2 = 0.6931471805599453
LOW = -1.0e30
SAFE_SUM = 1.0e-25
SAFE_TOP = 1.0e30

LANES = 128
STATE_TILE = 256
ROW_TILE = 416
DEPTH = 128
WEIGHT_AT = 96
SHIFT_AT = 99
LIVE_AT = 102


def split3(value):
    high = value.astype(jnp.bfloat16).astype(jnp.float32)
    rest = value - high
    middle = rest.astype(jnp.bfloat16).astype(jnp.float32)
    low = (rest - middle).astype(jnp.bfloat16).astype(jnp.float32)
    return high, middle, low


def live_rows(group, own, live_slots):
    lane = lax.broadcasted_iota(jnp.int32, (1, LANES), 1)
    tile = group + 16 * lax.shift_right_logical(lane, 3)
    slot = tile * LANES + 8 * own + lax.bitwise_and(lane, 7)
    return slot.astype(jnp.float32) < live_slots


def prepare_kernel(group_ref, anchor_hbm_ref, energy_ref, out_ref, anchor_ref, tile_ref, anchor_sems, sems):
    group = group_ref[0]
    tiles = tile_ref.shape[0]

    def fetch(i):
        at = pl.multiple_of((group + tiles * i) * LANES, LANES)
        return pltpu.make_async_copy(energy_ref.at[:, pl.ds(at, LANES)], tile_ref.at[i], sems.at[i])

    total = anchor_ref.shape[1]
    step = 4096

    def fetch_anchor(k):
        part = pl.ds(k * step, step)
        return pltpu.make_async_copy(anchor_hbm_ref.at[:, part], anchor_ref.at[:, part], anchor_sems.at[k])

    for k in range(total // step):
        fetch_anchor(k).start()
    for i in range(tiles):
        fetch(i).start()
    base = group * 16
    row = lax.broadcasted_iota(jnp.int32, (16, step), 0)
    counts = jnp.zeros((16, 16), jnp.float32)
    live = jnp.zeros((1, step), jnp.float32)
    for start in range(0, total, step):
        fetch_anchor(start // step).wait()
        anchor = anchor_ref[:, start : start + step]
        high = lax.shift_right_logical(anchor, 4) - base
        low = lax.bitwise_and(anchor, 15)
        high_hot = jnp.where(row == high, 1.0, 0.0).astype(jnp.bfloat16)
        low_hot = jnp.where(row == low, 1.0, 0.0).astype(jnp.bfloat16)
        live += jnp.where(anchor < tiles * STATE_TILE, 1.0, 0.0)
        counts += lax.dot_general(
            high_hot, low_hot, (((1,), (1,)), ((), ())), preferred_element_type=jnp.float32
        )
    lane = lax.broadcasted_iota(jnp.int32, (16, 256), 1)
    row16 = lax.broadcasted_iota(jnp.int32, (16, 256), 0)
    spread_out = jnp.where(lax.bitwise_and(lane, 15) == row16, 1.0, 0.0)
    placed = lax.dot_general(
        counts,
        spread_out,
        (((1,), (0,)), ((), ())),
        preferred_element_type=jnp.float32,
        precision=lax.Precision.HIGHEST,
    )
    flat = jnp.sum(jnp.where(lax.shift_right_logical(lane, 4) == row16, placed, 0.0), axis=0, keepdims=True)
    amount = jnp.broadcast_to(jnp.sum(live, axis=1, keepdims=True), (1, LANES))

    def halves(value):
        high = jnp.floor(value * (1.0 / 256.0))
        return high, value - high * 256.0

    flat_high, flat_low = halves(flat)
    rows = [flat_high[:, :LANES], flat_high[:, LANES:], flat_low[:, :LANES], flat_low[:, LANES:]]
    rows += list(halves(amount)) + [jnp.zeros((2, LANES), jnp.float32)]
    for i in range(tiles):
        fetch(i).wait()
    lane = lax.shift_right_logical(lax.broadcasted_iota(jnp.int32, tile_ref.shape[1:], 1), 3)
    energies = [tile_ref[i].astype(jnp.float32) for i in range(tiles)]
    for j in range(out_ref.shape[0]):
        piece = energies[j]
        for i in range(tiles):
            if i != j:
                piece = jnp.where(lane == i, pltpu.roll(energies[i], (8 * (i - j)) % LANES, 1), piece)
        out_ref[j] = jnp.concatenate([piece] + rows, axis=0).astype(jnp.bfloat16)


def prepare(group, anchor, energy, copies, groups):
    total = anchor.shape[0]
    components = energy.shape[0]
    hbm = pltpu.MemorySpace.HBM
    return pl.pallas_call(
        prepare_kernel,
        out_shape=jax.ShapeDtypeStruct((copies, components + 8, LANES), jnp.bfloat16),
        in_specs=[pl.BlockSpec(memory_space=pltpu.SMEM)] + [pl.BlockSpec(memory_space=hbm)] * 2,
        out_specs=pl.BlockSpec(memory_space=pltpu.VMEM),
        scratch_shapes=[
            pltpu.VMEM((1, total), jnp.int32),
            pltpu.VMEM((groups, components, LANES), jnp.bfloat16),
            pltpu.SemaphoreType.DMA((total // 4096,)),
            pltpu.SemaphoreType.DMA((groups,)),
        ],
        compiler_params=pltpu.CompilerParams(vmem_limit_bytes=8 * 2**20),
        name="prepare",
    )(
        group,
        pltpu.with_memory_space_constraint(anchor.reshape(1, total), hbm),
        pltpu.with_memory_space_constraint(energy, hbm),
    )


def arrange_kernel(group_ref, own_ref, pieces_ref, left_ref, amount_ref, wide_ref):
    components = pieces_ref.shape[1] - 8
    wide_ref[...] = jnp.zeros_like(wide_ref)
    lane = lax.broadcasted_iota(jnp.int32, (1, LANES), 1)
    row = lax.broadcasted_iota(jnp.int32, (DEPTH - 3 * components, LANES), 0)
    at = jnp.int32(0)
    for b in range(pieces_ref.shape[0]):
        piece = pieces_ref[b].astype(jnp.float32)
        rest = piece[components:]
        is_live = live_rows(group_ref[0], own_ref[0], rest[4:5] * 256.0 + rest[5:6])
        live = jnp.where(is_live, 1.0, 0.0)
        starts = jnp.where(lax.bitwise_and(lane, 7) == 0, live, 0.0)
        energy = piece[:components] * live
        tail = jnp.where(row < SHIFT_AT - WEIGHT_AT, 1.0, jnp.where(row == LIVE_AT - WEIGHT_AT, live, 0.0))
        block = jnp.concatenate([energy, energy, energy, tail], axis=0)
        wide_ref[pl.ds(pl.multiple_of(at, 8), LANES), :] = block.T
        at = at + 8 * jnp.sum(starts).astype(jnp.int32)
    left_ref[...] = wide_ref[...].astype(jnp.bfloat16)
    amount_ref[0] = at


def arrange(group, own, pieces):
    most = pl.cdiv(pieces.shape[0] * LANES, ROW_TILE) * ROW_TILE
    smem = pl.BlockSpec(memory_space=pltpu.SMEM)
    vmem = pl.BlockSpec(memory_space=pltpu.VMEM)
    return pl.pallas_call(
        arrange_kernel,
        out_shape=[
            jax.ShapeDtypeStruct((most, DEPTH), jnp.bfloat16),
            jax.ShapeDtypeStruct((1,), jnp.int32),
        ],
        in_specs=[smem, smem, vmem],
        out_specs=[vmem, smem],
        scratch_shapes=[pltpu.VMEM((most, DEPTH), jnp.float32)],
        compiler_params=pltpu.CompilerParams(vmem_limit_bytes=6 * 2**20),
        name="arrange",
    )(group, own, pieces)


def pack_kernel(pieces_ref, start_ref, coef_ref, out_ref):
    components = coef_ref.shape[0]
    counts = jnp.sum(pieces_ref[:, components:, :].astype(jnp.float32), axis=0)
    counts = jnp.concatenate([counts[0:1], counts[1:2]], axis=1) * 256.0 + jnp.concatenate(
        [counts[2:3], counts[3:4]], axis=1
    )
    rows = list(split3(jnp.log(counts))) + list(split3(start_ref[...]))
    rows.append(jnp.zeros((2, STATE_TILE), jnp.float32))
    packed = jnp.concatenate([coef_ref[...].astype(jnp.float32)] + rows, axis=0).astype(jnp.bfloat16)
    out_ref[...] = jnp.broadcast_to(packed[None], out_ref.shape)


def pack(pieces, f_start, coef, copies):
    components, states = coef.shape
    return pl.pallas_call(
        pack_kernel,
        out_shape=jax.ShapeDtypeStruct((copies, components + 8, states), jnp.bfloat16),
        compiler_params=pltpu.CompilerParams(vmem_limit_bytes=4 * 2**20),
        name="pack",
    )(pieces, f_start.reshape(1, states), coef)


def merge_logs(parts):
    highest = jnp.max(parts, axis=0)
    return highest + jnp.log2(jnp.sum(jnp.exp2(parts - highest[None]), axis=0))


def merge_pair_kernel(kept_ref, other_ref, out_ref):
    kept = kept_ref[...]
    other = other_ref[...]
    highest = jnp.maximum(kept, other)
    value = highest + jnp.log2(jnp.exp2(kept - highest) + jnp.exp2(other - highest))
    out_ref[...] = jnp.broadcast_to(value[None], out_ref.shape)


def merge_pair(kept, other, copies):
    return pl.pallas_call(
        merge_pair_kernel,
        out_shape=jax.ShapeDtypeStruct((copies,) + kept.shape, jnp.float32),
        compiler_params=pltpu.CompilerParams(vmem_limit_bytes=4 * 2**20),
        name="merge_pair",
    )(kept, other)


def merge_kernel(parts_ref, out_ref):
    out_ref[...] = jnp.broadcast_to(merge_logs(parts_ref[...])[None], out_ref.shape)


def merge(parts, copies):
    return pl.pallas_call(
        merge_kernel,
        out_shape=jax.ShapeDtypeStruct((copies,) + parts.shape[1:], jnp.float32),
        compiler_params=pltpu.CompilerParams(vmem_limit_bytes=4 * 2**20),
        name="merge",
    )(parts)


def centered(value):
    mean = jnp.sum(jnp.sum(value, axis=1, keepdims=True), axis=0, keepdims=True) / value.size
    return value - mean


def largest(value):
    return jnp.max(jnp.max(value, axis=1, keepdims=True), axis=0, keepdims=True)


def folded(value, combine):
    return combine(value[:, :LANES], value[:, LANES:])


def sweep_kernel(first, *refs):
    if first:
        amount_ref, own_ref, packed_ref, left_ref, kept_ref, sent_ref, wide_ref, shifted_ref, right_ref, scaled_ref, acc_ref, some_ref, tall_ref, top_ref = refs
        source_ref = shifted_ref
    else:
        amount_ref, own_ref, packed_ref, left_ref, parts_ref, old_ref, kept_ref, sent_ref, wide_ref, some_ref, right_ref, scaled_ref, acc_ref, tall_ref, top_ref = refs
        source_ref = left_ref
    groups, packed_rows, _ = packed_ref.shape
    components = packed_rows - 8
    states = groups * STATE_TILE
    pair = STATE_TILE // LANES
    amount = amount_ref[0]
    tiles = (amount + ROW_TILE - 1) // ROW_TILE

    for g in range(groups):
        rows = packed_ref[g, components:, :].astype(jnp.float32)
        log_counts = rows[0:1] + rows[1:2] + rows[2:3]
        value = log_counts + (rows[3:4] + rows[4:5] + rows[5:6]) if first else log_counts
        for h in range(pair):
            wide_ref[pair * g + h : pair * g + h + 1, :] = value[:, h * LANES : (h + 1) * LANES]
    if first:
        weights = wide_ref[...]
    else:
        raw = old_ref[...] - merge_logs(parts_ref[...]) * LN2
        wide = wide_ref[...] + centered(raw)
        wide_ref[...] = wide
        weights = wide - largest(wide - old_ref[...])
    w0, w1, w2 = split3(weights * LOG2E)

    row = lax.broadcasted_iota(jnp.int32, (DEPTH - 3 * components, LANES), 0)
    ones = jnp.where(row < LIVE_AT - WEIGHT_AT, 1.0, 0.0)
    for g in range(groups):
        coef = packed_ref[g, :components, :].astype(jnp.float32) * (-LOG2E)
        lanes = slice(g * STATE_TILE, (g + 1) * STATE_TILE)
        for k, part in enumerate(split3(coef)):
            right_ref[k * components : (k + 1) * components, lanes] = part.astype(jnp.bfloat16)
        for h in range(pair):
            at = pair * g + h
            tail = jnp.where(row == 0, w0[at : at + 1], jnp.where(row == 1, w1[at : at + 1], jnp.where(row == 2, w2[at : at + 1], ones)))
            right_ref[WEIGHT_AT:, at * LANES : (at + 1) * LANES] = tail.astype(jnp.bfloat16)

    def product(left, right):
        return lax.dot_general(left, right, (((1,), (0,)), ((), ())), preferred_element_type=jnp.float32)

    if first:
        lane = lax.broadcasted_iota(jnp.int32, (DEPTH, LANES), 1)
        for h in range(2):
            some = jnp.zeros((DEPTH, LANES), jnp.float32)
            for j in range(8):
                g = 8 * h + j
                tile = right_ref[:, g * STATE_TILE : g * STATE_TILE + LANES].astype(jnp.float32)
                moved = tile if j == 0 else pltpu.roll(tile, 16 * j, 1)
                some = jnp.where(lax.shift_right_logical(lane, 4) == j, moved, some)
            some_ref[:, h * LANES : (h + 1) * LANES] = some.astype(jnp.bfloat16)

    acc_ref[...] = jnp.zeros_like(acc_ref)
    lane = lax.broadcasted_iota(jnp.int32, (ROW_TILE, LANES), 1)

    def shifted(block, shift):
        s0, s1, s2 = split3(-shift)
        values = jnp.where(lane == SHIFT_AT, s0, jnp.where(lane == SHIFT_AT + 1, s1, s2))
        chosen = jnp.logical_and(lane >= SHIFT_AT, lane < LIVE_AT)
        return jnp.where(chosen, values, block.astype(jnp.float32)).astype(jnp.bfloat16)

    def visit(t, carry):
        least, most = carry
        rows = pl.ds(pl.multiple_of(t * ROW_TILE, ROW_TILE), ROW_TILE)
        left = left_ref[rows, :]
        if first:
            sampled = folded(product(left, some_ref[...]), jnp.maximum)
            shift = jnp.max(sampled, axis=1, keepdims=True)
            left = shifted(left, shift)
        live = left_ref[rows, LIVE_AT : LIVE_AT + 1].astype(jnp.float32)
        total = jnp.zeros((ROW_TILE, LANES), jnp.float32)
        for g in range(groups):
            lanes = slice(g * STATE_TILE, (g + 1) * STATE_TILE)
            scaled = jnp.exp2(product(left, right_ref[:, lanes]))
            scaled_ref[:, lanes] = scaled
            total += folded(scaled, jnp.add)
        denominator = jnp.sum(total, axis=1, keepdims=True)
        least = jnp.minimum(least, jnp.where(live > 0.0, denominator, 1.0))
        most = jnp.maximum(most, jnp.where(live > 0.0, denominator, 1.0))
        share = jnp.broadcast_to(live / denominator, (ROW_TILE, LANES))
        if first:
            shifted_ref[rows, :] = shifted(left, shift + jnp.log2(denominator))
        for k in range(states // LANES):
            lanes = slice(k * LANES, (k + 1) * LANES)
            part = scaled_ref[:, lanes] * share
            acc_ref[:, lanes] += jnp.sum(part.reshape(ROW_TILE // 8, 8, LANES), axis=0)
        return least, most

    unit = jnp.ones((ROW_TILE, 1), jnp.float32)
    least, most = lax.fori_loop(0, tiles, visit, (unit, unit))
    least = jnp.min(least, axis=0, keepdims=True)
    most = jnp.max(most, axis=0, keepdims=True)
    sums = jnp.sum(acc_ref[...], axis=0, keepdims=True)
    smallest = jnp.min(sums, axis=1, keepdims=True)
    logs = jnp.where(sums > 0.0, jnp.log2(jnp.maximum(sums, SAFE_SUM)), LOW)

    def give(value):
        for k in range(states // LANES):
            tall_ref[k : k + 1, :] = value[:, k * LANES : (k + 1) * LANES]
        half = kept_ref.shape[0]
        core = lax.rem(own_ref[0], 2)
        kept_ref[...] = tall_ref[pl.ds(pl.multiple_of(core * half, half), half), :]
        sent_ref[...] = tall_ref[pl.ds(pl.multiple_of((1 - core) * half, half), half), :]

    give(logs)
    enough = jnp.logical_and(smallest >= SAFE_SUM, smallest * least >= SAFE_SUM)
    safe = jnp.logical_and(enough, jnp.logical_and(most < SAFE_TOP, least > SAFE_SUM))
    unsafe = jnp.max(jnp.where(safe, 0.0, 1.0)) > 0.0

    @pl.when(jnp.logical_and(amount > 0, unsafe))
    def exact():
        acc_ref[...] = jnp.zeros_like(acc_ref)
        top_ref[...] = jnp.full_like(top_ref, LOW)

        def tile_at(k):
            return pl.ds(pl.multiple_of(k * LANES, LANES), LANES)

        def slots(t, carry):
            rows = pl.ds(pl.multiple_of(t * ROW_TILE, ROW_TILE), ROW_TILE)
            left = left_ref[rows, :]
            is_live = jnp.broadcast_to(left[:, LIVE_AT : LIVE_AT + 1].astype(jnp.float32), (ROW_TILE, LANES)) > 0.0

            def column(k, pieces):
                high, total = pieces
                score = product(left, right_ref[:, tile_at(k)])
                newer = jnp.maximum(high, score)
                return newer, total * jnp.exp2(high - newer) + jnp.exp2(score - newer)

            start = (jnp.full((ROW_TILE, LANES), LOW, jnp.float32), jnp.zeros((ROW_TILE, LANES), jnp.float32))
            high, total = lax.fori_loop(0, states // LANES, column, start)
            top = jnp.max(high, axis=1, keepdims=True)
            total = jnp.sum(total * jnp.exp2(high - top), axis=1, keepdims=True)
            norm = top + jnp.log2(total)
            if first:
                shifted_ref[rows, :] = shifted(left, norm)

            def state(k, inner):
                lanes = tile_at(k)
                term = jnp.where(is_live, product(left, right_ref[:, lanes]) - norm, LOW)
                older = top_ref[:, lanes]
                newer = jnp.maximum(older, jnp.max(term, axis=0, keepdims=True))
                added = jnp.sum(jnp.where(is_live, jnp.exp2(term - newer), 0.0), axis=0, keepdims=True)
                acc_ref[0:1, lanes] = acc_ref[0:1, lanes] * jnp.exp2(older - newer) + added
                top_ref[:, lanes] = newer
                return inner

            return lax.fori_loop(0, states // LANES, state, carry)

        lax.fori_loop(0, tiles, slots, 0)
        give(top_ref[...] + jnp.log2(acc_ref[0:1, :]))


def sweep(amount, own, packed, left, parts, old):
    groups = packed.shape[0]
    states = groups * STATE_TILE
    first = parts is None
    tall = states // LANES
    operands = [amount, own, packed, left] + ([] if first else [parts, old])
    outs = [((tall // 2, LANES), jnp.float32)] * 2 + [((tall, LANES), jnp.float32)]
    scratch = [
        pltpu.VMEM((DEPTH, states), jnp.bfloat16),
        pltpu.VMEM((ROW_TILE, states), jnp.float32),
        pltpu.VMEM((8, states), jnp.float32),
        pltpu.VMEM((DEPTH, 2 * LANES), jnp.bfloat16),
        pltpu.VMEM((tall, LANES), jnp.float32),
        pltpu.VMEM((1, states), jnp.float32),
    ]
    if first:
        outs.append((left.shape, jnp.bfloat16))
    else:
        scratch = [scratch[3]] + scratch[:3] + scratch[4:]
    return pl.pallas_call(
        functools.partial(sweep_kernel, first),
        out_shape=[jax.ShapeDtypeStruct(*out) for out in outs],
        in_specs=[pl.BlockSpec(memory_space=pltpu.SMEM)] * 2 + [pl.BlockSpec(memory_space=pltpu.VMEM)] * (len(operands) - 2),
        scratch_shapes=scratch,
        compiler_params=pltpu.CompilerParams(vmem_limit_bytes=20 * 2**20),
        name="first_sweep" if first else "next_sweep",
    )(*operands)


def finish_kernel(group_ref, parts_ref, old_ref, out_ref, hold_ref):
    raw = old_ref[...] - merge_logs(parts_ref[...]) * LN2
    hold_ref[...] = centered(raw)
    out_ref[...] = hold_ref[pl.ds(group_ref[0] * out_ref.shape[0], out_ref.shape[0]), :]


def finish(group, parts, old):
    rows = old.shape[0] // parts.shape[0]
    return pl.pallas_call(
        finish_kernel,
        out_shape=jax.ShapeDtypeStruct((rows, LANES), jnp.float32),
        grid_spec=pltpu.PrefetchScalarGridSpec(
            num_scalar_prefetch=1,
            grid=(1,),
            in_specs=[
                pl.BlockSpec(parts.shape, lambda i, g: (0, 0, 0)),
                pl.BlockSpec(old.shape, lambda i, g: (0, 0)),
            ],
            out_specs=pl.BlockSpec((rows, LANES), lambda i, g: (0, 0)),
            scratch_shapes=[pltpu.VMEM(old.shape, jnp.float32)],
        ),
        compiler_params=pltpu.CompilerParams(vmem_limit_bytes=4 * 2**20),
        name="finish",
    )(group, parts, old)


def spread(copies, axis, members=None):
    return lax.all_to_all(copies, axis, 0, 0, axis_index_groups=members)


def merged(kept, sent, groups, blocks):
    chips = blocks // 2
    other = lax.ppermute(sent, "sample", [(i, i ^ 1) for i in range(blocks)])
    lines = [[2 * z + core for z in range(chips)] for core in range(2)]
    along = spread(merge_pair(kept, other, chips), "sample", lines)
    planes = [[blocks * s + 2 * z + core for s in range(groups) for core in range(2)] for z in range(chips)]
    parts = spread(merge(along, 2 * groups), ("state", "sample"), planes)
    return parts.reshape(groups, 2 * kept.shape[0], LANES)


def per_device(energy, coef, anchor, f_start):
    groups = lax.axis_size("state")
    blocks = lax.axis_size("sample")
    group = lax.axis_index("state").astype(jnp.int32).reshape(1)
    own = lax.axis_index("sample").astype(jnp.int32).reshape(1)
    pieces = spread(prepare(group, anchor, energy, blocks, groups), "sample")
    packed = spread(pack(pieces, f_start, coef, groups), "state")
    left, amount = arrange(group, own, pieces)
    parts = None
    weights = None
    for iteration in range(ITERS):
        kept, sent, weights, *rest = sweep(amount, own, packed, left, parts, weights)
        if rest:
            left = rest[0]
        parts = merged(kept, sent, groups, blocks)
    return finish(group, parts, weights).reshape(-1)


def solution(mesh):
    in_specs = (P(None, "sample"), P(None, "state"), P("sample"), P("state"))
    out_specs = P("state")
    return jax.shard_map(
        per_device, mesh=mesh, in_specs=in_specs, out_specs=out_specs, check_vma=False
    )
```

```python
import functools

import jax
import jax.numpy as jnp
from jax import lax
from jax.experimental import pallas as pl
from jax.experimental.pallas import tpu as pltpu
from jax.sharding import PartitionSpec as P

ITERS = 2

LOG2E = 1.4426950408889634
LN2 = 0.6931471805599453
LOW = -1.0e30
SAFE_SUM = 1.0e-25
SAFE_TOP = 1.0e30

LANES = 128
STATE_TILE = 256
ROW_TILE = 416
DEPTH = 128
WEIGHT_AT = 96
SHIFT_AT = 99
LIVE_AT = 102


def split3(value):
    high = value.astype(jnp.bfloat16).astype(jnp.float32)
    rest = value - high
    middle = rest.astype(jnp.bfloat16).astype(jnp.float32)
    low = (rest - middle).astype(jnp.bfloat16).astype(jnp.float32)
    return high, middle, low


def live_rows(group, own, live_slots):
    lane = lax.broadcasted_iota(jnp.int32, (1, LANES), 1)
    tile = group + 16 * lax.shift_right_logical(lane, 3)
    slot = tile * LANES + 8 * own + lax.bitwise_and(lane, 7)
    return slot.astype(jnp.float32) < live_slots


def prepare_kernel(group_ref, anchor_hbm_ref, energy_ref, out_ref, anchor_ref, tile_ref, anchor_sems, sems):
    group = group_ref[0]
    tiles = tile_ref.shape[0]

    def fetch(i):
        at = pl.multiple_of((group + tiles * i) * LANES, LANES)
        return pltpu.make_async_copy(energy_ref.at[:, pl.ds(at, LANES)], tile_ref.at[i], sems.at[i])

    total = anchor_ref.shape[1]
    step = 4096

    def fetch_anchor(k):
        part = pl.ds(k * step, step)
        return pltpu.make_async_copy(anchor_hbm_ref.at[:, part], anchor_ref.at[:, part], anchor_sems.at[k])

    for k in range(total // step):
        fetch_anchor(k).start()
    for i in range(tiles):
        fetch(i).start()
    base = group * 16
    row = lax.broadcasted_iota(jnp.int32, (16, step), 0)
    counts = jnp.zeros((16, 16), jnp.float32)
    live = jnp.zeros((1, step), jnp.float32)
    for start in range(0, total, step):
        fetch_anchor(start // step).wait()
        anchor = anchor_ref[:, start : start + step]
        high = lax.shift_right_logical(anchor, 4) - base
        low = lax.bitwise_and(anchor, 15)
        high_hot = jnp.where(row == high, 1.0, 0.0).astype(jnp.bfloat16)
        low_hot = jnp.where(row == low, 1.0, 0.0).astype(jnp.bfloat16)
        live += jnp.where(anchor < tiles * STATE_TILE, 1.0, 0.0)
        counts += lax.dot_general(
            high_hot, low_hot, (((1,), (1,)), ((), ())), preferred_element_type=jnp.float32
        )
    lane = lax.broadcasted_iota(jnp.int32, (16, 256), 1)
    row16 = lax.broadcasted_iota(jnp.int32, (16, 256), 0)
    spread_out = jnp.where(lax.bitwise_and(lane, 15) == row16, 1.0, 0.0)
    placed = lax.dot_general(
        counts,
        spread_out,
        (((1,), (0,)), ((), ())),
        preferred_element_type=jnp.float32,
        precision=lax.Precision.HIGHEST,
    )
    flat = jnp.sum(jnp.where(lax.shift_right_logical(lane, 4) == row16, placed, 0.0), axis=0, keepdims=True)
    amount = jnp.broadcast_to(jnp.sum(live, axis=1, keepdims=True), (1, LANES))

    def halves(value):
        high = jnp.floor(value * (1.0 / 256.0))
        return high, value - high * 256.0

    flat_high, flat_low = halves(flat)
    rows = [flat_high[:, :LANES], flat_high[:, LANES:], flat_low[:, :LANES], flat_low[:, LANES:]]
    rows += list(halves(amount)) + [jnp.zeros((2, LANES), jnp.float32)]
    for i in range(tiles):
        fetch(i).wait()
    lane = lax.shift_right_logical(lax.broadcasted_iota(jnp.int32, tile_ref.shape[1:], 1), 3)
    energies = [tile_ref[i].astype(jnp.float32) for i in range(tiles)]
    for j in range(out_ref.shape[0]):
        piece = energies[j]
        for i in range(tiles):
            if i != j:
                piece = jnp.where(lane == i, pltpu.roll(energies[i], (8 * (i - j)) % LANES, 1), piece)
        out_ref[j] = jnp.concatenate([piece] + rows, axis=0).astype(jnp.bfloat16)


def prepare(group, anchor, energy, copies, groups):
    total = anchor.shape[0]
    components = energy.shape[0]
    hbm = pltpu.MemorySpace.HBM
    return pl.pallas_call(
        prepare_kernel,
        out_shape=jax.ShapeDtypeStruct((copies, components + 8, LANES), jnp.bfloat16),
        in_specs=[pl.BlockSpec(memory_space=pltpu.SMEM)] + [pl.BlockSpec(memory_space=hbm)] * 2,
        out_specs=pl.BlockSpec(memory_space=pltpu.VMEM),
        scratch_shapes=[
            pltpu.VMEM((1, total), jnp.int32),
            pltpu.VMEM((groups, components, LANES), jnp.bfloat16),
            pltpu.SemaphoreType.DMA((total // 4096,)),
            pltpu.SemaphoreType.DMA((groups,)),
        ],
        compiler_params=pltpu.CompilerParams(vmem_limit_bytes=8 * 2**20),
        name="prepare",
    )(
        group,
        pltpu.with_memory_space_constraint(anchor.reshape(1, total), hbm),
        pltpu.with_memory_space_constraint(energy, hbm),
    )


def arrange_kernel(group_ref, own_ref, pieces_ref, left_ref, amount_ref, wide_ref):
    components = pieces_ref.shape[1] - 8
    wide_ref[...] = jnp.zeros_like(wide_ref)
    lane = lax.broadcasted_iota(jnp.int32, (1, LANES), 1)
    row = lax.broadcasted_iota(jnp.int32, (DEPTH - 3 * components, LANES), 0)
    at = jnp.int32(0)
    for b in range(pieces_ref.shape[0]):
        piece = pieces_ref[b].astype(jnp.float32)
        rest = piece[components:]
        is_live = live_rows(group_ref[0], own_ref[0], rest[4:5] * 256.0 + rest[5:6])
        live = jnp.where(is_live, 1.0, 0.0)
        starts = jnp.where(lax.bitwise_and(lane, 7) == 0, live, 0.0)
        energy = piece[:components] * live
        tail = jnp.where(row < SHIFT_AT - WEIGHT_AT, 1.0, jnp.where(row == LIVE_AT - WEIGHT_AT, live, 0.0))
        block = jnp.concatenate([energy, energy, energy, tail], axis=0)
        wide_ref[pl.ds(pl.multiple_of(at, 8), LANES), :] = block.T
        at = at + 8 * jnp.sum(starts).astype(jnp.int32)
    left_ref[...] = wide_ref[...].astype(jnp.bfloat16)
    amount_ref[0] = at


def arrange(group, own, pieces):
    most = pl.cdiv(pieces.shape[0] * LANES, ROW_TILE) * ROW_TILE
    smem = pl.BlockSpec(memory_space=pltpu.SMEM)
    vmem = pl.BlockSpec(memory_space=pltpu.VMEM)
    return pl.pallas_call(
        arrange_kernel,
        out_shape=[
            jax.ShapeDtypeStruct((most, DEPTH), jnp.bfloat16),
            jax.ShapeDtypeStruct((1,), jnp.int32),
        ],
        in_specs=[smem, smem, vmem],
        out_specs=[vmem, smem],
        scratch_shapes=[pltpu.VMEM((most, DEPTH), jnp.float32)],
        compiler_params=pltpu.CompilerParams(vmem_limit_bytes=6 * 2**20),
        name="arrange",
    )(group, own, pieces)


def pack_kernel(pieces_ref, start_ref, coef_ref, out_ref):
    components = coef_ref.shape[0]
    counts = jnp.sum(pieces_ref[:, components:, :].astype(jnp.float32), axis=0)
    counts = jnp.concatenate([counts[0:1], counts[1:2]], axis=1) * 256.0 + jnp.concatenate(
        [counts[2:3], counts[3:4]], axis=1
    )
    rows = list(split3(jnp.log(counts))) + list(split3(start_ref[...]))
    rows.append(jnp.zeros((2, STATE_TILE), jnp.float32))
    packed = jnp.concatenate([coef_ref[...].astype(jnp.float32)] + rows, axis=0).astype(jnp.bfloat16)
    out_ref[...] = jnp.broadcast_to(packed[None], out_ref.shape)


def pack(pieces, f_start, coef, copies):
    components, states = coef.shape
    return pl.pallas_call(
        pack_kernel,
        out_shape=jax.ShapeDtypeStruct((copies, components + 8, states), jnp.bfloat16),
        compiler_params=pltpu.CompilerParams(vmem_limit_bytes=4 * 2**20),
        name="pack",
    )(pieces, f_start.reshape(1, states), coef)


def merge_logs(parts):
    highest = jnp.max(parts, axis=0)
    return highest + jnp.log2(jnp.sum(jnp.exp2(parts - highest[None]), axis=0))


def merge_pair_kernel(kept_ref, other_ref, out_ref):
    kept = kept_ref[...]
    other = other_ref[...]
    highest = jnp.maximum(kept, other)
    value = highest + jnp.log2(jnp.exp2(kept - highest) + jnp.exp2(other - highest))
    out_ref[...] = jnp.broadcast_to(value[None], out_ref.shape)


def merge_pair(kept, other, copies):
    return pl.pallas_call(
        merge_pair_kernel,
        out_shape=jax.ShapeDtypeStruct((copies,) + kept.shape, jnp.float32),
        compiler_params=pltpu.CompilerParams(vmem_limit_bytes=4 * 2**20),
        name="merge_pair",
    )(kept, other)


def merge_kernel(parts_ref, out_ref):
    out_ref[...] = jnp.broadcast_to(merge_logs(parts_ref[...])[None], out_ref.shape)


def merge(parts, copies):
    return pl.pallas_call(
        merge_kernel,
        out_shape=jax.ShapeDtypeStruct((copies,) + parts.shape[1:], jnp.float32),
        compiler_params=pltpu.CompilerParams(vmem_limit_bytes=4 * 2**20),
        name="merge",
    )(parts)


def centered(value):
    mean = jnp.sum(jnp.sum(value, axis=1, keepdims=True), axis=0, keepdims=True) / value.size
    return value - mean


def largest(value):
    return jnp.max(jnp.max(value, axis=1, keepdims=True), axis=0, keepdims=True)


def folded(value, combine):
    return combine(value[:, :LANES], value[:, LANES:])


def sweep_kernel(first, *refs):
    if first:
        amount_ref, own_ref, packed_ref, left_ref, kept_ref, sent_ref, wide_ref, shifted_ref, right_ref, scaled_ref, acc_ref, some_ref, tall_ref, top_ref = refs
        source_ref = shifted_ref
    else:
        amount_ref, own_ref, packed_ref, left_ref, parts_ref, old_ref, kept_ref, sent_ref, wide_ref, some_ref, right_ref, scaled_ref, acc_ref, tall_ref, top_ref = refs
        source_ref = left_ref
    groups, packed_rows, _ = packed_ref.shape
    components = packed_rows - 8
    states = groups * STATE_TILE
    pair = STATE_TILE // LANES
    amount = amount_ref[0]
    tiles = (amount + ROW_TILE - 1) // ROW_TILE

    for g in range(groups):
        rows = packed_ref[g, components:, :].astype(jnp.float32)
        log_counts = rows[0:1] + rows[1:2] + rows[2:3]
        value = log_counts + (rows[3:4] + rows[4:5] + rows[5:6]) if first else log_counts
        for h in range(pair):
            wide_ref[pair * g + h : pair * g + h + 1, :] = value[:, h * LANES : (h + 1) * LANES]
    if first:
        weights = wide_ref[...]
    else:
        raw = old_ref[...] - merge_logs(parts_ref[...]) * LN2
        wide = wide_ref[...] + centered(raw)
        wide_ref[...] = wide
        weights = wide - largest(wide - old_ref[...])
    w0, w1, w2 = split3(weights * LOG2E)

    row = lax.broadcasted_iota(jnp.int32, (DEPTH - 3 * components, LANES), 0)
    ones = jnp.where(row < LIVE_AT - WEIGHT_AT, 1.0, 0.0)
    for g in range(groups):
        coef = packed_ref[g, :components, :].astype(jnp.float32) * (-LOG2E)
        lanes = slice(g * STATE_TILE, (g + 1) * STATE_TILE)
        for k, part in enumerate(split3(coef)):
            right_ref[k * components : (k + 1) * components, lanes] = part.astype(jnp.bfloat16)
        for h in range(pair):
            at = pair * g + h
            tail = jnp.where(row == 0, w0[at : at + 1], jnp.where(row == 1, w1[at : at + 1], jnp.where(row == 2, w2[at : at + 1], ones)))
            right_ref[WEIGHT_AT:, at * LANES : (at + 1) * LANES] = tail.astype(jnp.bfloat16)

    def product(left, right):
        return lax.dot_general(left, right, (((1,), (0,)), ((), ())), preferred_element_type=jnp.float32)

    if first:
        lane = lax.broadcasted_iota(jnp.int32, (DEPTH, LANES), 1)
        for h in range(2):
            some = jnp.zeros((DEPTH, LANES), jnp.float32)
            for j in range(8):
                g = 8 * h + j
                tile = right_ref[:, g * STATE_TILE : g * STATE_TILE + LANES].astype(jnp.float32)
                moved = tile if j == 0 else pltpu.roll(tile, 16 * j, 1)
                some = jnp.where(lax.shift_right_logical(lane, 4) == j, moved, some)
            some_ref[:, h * LANES : (h + 1) * LANES] = some.astype(jnp.bfloat16)

    acc_ref[...] = jnp.zeros_like(acc_ref)
    lane = lax.broadcasted_iota(jnp.int32, (ROW_TILE, LANES), 1)

    def shifted(block, shift):
        s0, s1, s2 = split3(-shift)
        values = jnp.where(lane == SHIFT_AT, s0, jnp.where(lane == SHIFT_AT + 1, s1, s2))
        chosen = jnp.logical_and(lane >= SHIFT_AT, lane < LIVE_AT)
        return jnp.where(chosen, values, block.astype(jnp.float32)).astype(jnp.bfloat16)

    def visit(t, carry):
        least, most = carry
        rows = pl.ds(pl.multiple_of(t * ROW_TILE, ROW_TILE), ROW_TILE)
        left = left_ref[rows, :]
        if first:
            sampled = folded(product(left, some_ref[...]), jnp.maximum)
            shift = jnp.max(sampled, axis=1, keepdims=True)
            left = shifted(left, shift)
        live = left_ref[rows, LIVE_AT : LIVE_AT + 1].astype(jnp.float32)
        total = jnp.zeros((ROW_TILE, LANES), jnp.float32)
        for g in range(groups):
            lanes = slice(g * STATE_TILE, (g + 1) * STATE_TILE)
            scaled = jnp.exp2(product(left, right_ref[:, lanes]))
            scaled_ref[:, lanes] = scaled
            total += folded(scaled, jnp.add)
        denominator = jnp.sum(total, axis=1, keepdims=True)
        least = jnp.minimum(least, jnp.where(live > 0.0, denominator, 1.0))
        most = jnp.maximum(most, jnp.where(live > 0.0, denominator, 1.0))
        share = jnp.broadcast_to(live / denominator, (ROW_TILE, LANES))
        if first:
            shifted_ref[rows, :] = shifted(left, shift + jnp.log2(denominator))
        for k in range(states // LANES):
            lanes = slice(k * LANES, (k + 1) * LANES)
            part = scaled_ref[:, lanes] * share
            acc_ref[:, lanes] += jnp.sum(part.reshape(ROW_TILE // 8, 8, LANES), axis=0)
        return least, most

    unit = jnp.ones((ROW_TILE, 1), jnp.float32)
    least, most = lax.fori_loop(0, tiles, visit, (unit, unit))
    least = jnp.min(least, axis=0, keepdims=True)
    most = jnp.max(most, axis=0, keepdims=True)
    sums = jnp.sum(acc_ref[...], axis=0, keepdims=True)
    smallest = jnp.min(sums, axis=1, keepdims=True)
    logs = jnp.where(sums > 0.0, jnp.log2(jnp.maximum(sums, SAFE_SUM)), LOW)

    def give(value):
        for k in range(states // LANES):
            tall_ref[k : k + 1, :] = value[:, k * LANES : (k + 1) * LANES]
        half = kept_ref.shape[0]
        core = lax.rem(own_ref[0], 2)
        kept_ref[...] = tall_ref[pl.ds(pl.multiple_of(core * half, half), half), :]
        sent_ref[...] = tall_ref[pl.ds(pl.multiple_of((1 - core) * half, half), half), :]

    give(logs)
    enough = jnp.logical_and(smallest >= SAFE_SUM, smallest * least >= SAFE_SUM)
    safe = jnp.logical_and(enough, jnp.logical_and(most < SAFE_TOP, least > SAFE_SUM))
    unsafe = jnp.max(jnp.where(safe, 0.0, 1.0)) > 0.0

    @pl.when(jnp.logical_and(amount > 0, unsafe))
    def exact():
        acc_ref[...] = jnp.zeros_like(acc_ref)
        top_ref[...] = jnp.full_like(top_ref, LOW)

        def tile_at(k):
            return pl.ds(pl.multiple_of(k * LANES, LANES), LANES)

        def slots(t, carry):
            rows = pl.ds(pl.multiple_of(t * ROW_TILE, ROW_TILE), ROW_TILE)
            left = left_ref[rows, :]
            is_live = jnp.broadcast_to(left[:, LIVE_AT : LIVE_AT + 1].astype(jnp.float32), (ROW_TILE, LANES)) > 0.0

            def column(k, pieces):
                high, total = pieces
                score = product(left, right_ref[:, tile_at(k)])
                newer = jnp.maximum(high, score)
                return newer, total * jnp.exp2(high - newer) + jnp.exp2(score - newer)

            start = (jnp.full((ROW_TILE, LANES), LOW, jnp.float32), jnp.zeros((ROW_TILE, LANES), jnp.float32))
            high, total = lax.fori_loop(0, states // LANES, column, start)
            top = jnp.max(high, axis=1, keepdims=True)
            total = jnp.sum(total * jnp.exp2(high - top), axis=1, keepdims=True)
            norm = top + jnp.log2(total)
            if first:
                shifted_ref[rows, :] = shifted(left, norm)

            def state(k, inner):
                lanes = tile_at(k)
                term = jnp.where(is_live, product(left, right_ref[:, lanes]) - norm, LOW)
                older = top_ref[:, lanes]
                newer = jnp.maximum(older, jnp.max(term, axis=0, keepdims=True))
                added = jnp.sum(jnp.where(is_live, jnp.exp2(term - newer), 0.0), axis=0, keepdims=True)
                acc_ref[0:1, lanes] = acc_ref[0:1, lanes] * jnp.exp2(older - newer) + added
                top_ref[:, lanes] = newer
                return inner

            return lax.fori_loop(0, states // LANES, state, carry)

        lax.fori_loop(0, tiles, slots, 0)
        give(top_ref[...] + jnp.log2(acc_ref[0:1, :]))


def sweep(amount, own, packed, left, parts, old):
    groups = packed.shape[0]
    states = groups * STATE_TILE
    first = parts is None
    tall = states // LANES
    operands = [amount, own, packed, left] + ([] if first else [parts, old])
    outs = [((tall // 2, LANES), jnp.float32)] * 2 + [((tall, LANES), jnp.float32)]
    scratch = [
        pltpu.VMEM((DEPTH, states), jnp.bfloat16),
        pltpu.VMEM((ROW_TILE, states), jnp.float32),
        pltpu.VMEM((8, states), jnp.float32),
        pltpu.VMEM((DEPTH, 2 * LANES), jnp.bfloat16),
        pltpu.VMEM((tall, LANES), jnp.float32),
        pltpu.VMEM((1, states), jnp.float32),
    ]
    if first:
        outs.append((left.shape, jnp.bfloat16))
    else:
        scratch = [scratch[3]] + scratch[:3] + scratch[4:]
    return pl.pallas_call(
        functools.partial(sweep_kernel, first),
        out_shape=[jax.ShapeDtypeStruct(*out) for out in outs],
        in_specs=[pl.BlockSpec(memory_space=pltpu.SMEM)] * 2 + [pl.BlockSpec(memory_space=pltpu.VMEM)] * (len(operands) - 2),
        scratch_shapes=scratch,
        compiler_params=pltpu.CompilerParams(vmem_limit_bytes=20 * 2**20),
        name="first_sweep" if first else "next_sweep",
    )(*operands)


def finish_kernel(group_ref, parts_ref, old_ref, out_ref, hold_ref):
    raw = old_ref[...] - merge_logs(parts_ref[...]) * LN2
    hold_ref[...] = centered(raw)
    out_ref[...] = hold_ref[pl.ds(group_ref[0] * out_ref.shape[0], out_ref.shape[0]), :]


def finish(group, parts, old, groups):
    rows = old.shape[0] // groups
    return pl.pallas_call(
        finish_kernel,
        out_shape=jax.ShapeDtypeStruct((rows, LANES), jnp.float32),
        grid_spec=pltpu.PrefetchScalarGridSpec(
            num_scalar_prefetch=1,
            grid=(1,),
            in_specs=[
                pl.BlockSpec(parts.shape, lambda i, g: (0, 0, 0)),
                pl.BlockSpec(old.shape, lambda i, g: (0, 0)),
            ],
            out_specs=pl.BlockSpec((rows, LANES), lambda i, g: (0, 0)),
            scratch_shapes=[pltpu.VMEM(old.shape, jnp.float32)],
        ),
        compiler_params=pltpu.CompilerParams(vmem_limit_bytes=4 * 2**20),
        name="finish",
    )(group, parts, old)


def spread(copies, axis):
    return lax.all_to_all(copies, axis, 0, 0)


def merged(kept, sent, groups, blocks):
    other = lax.ppermute(sent, "sample", [(i, i ^ 1) for i in range(blocks)])
    across = spread(merge_pair(kept, other, groups), "state")
    parts = spread(merge(across, blocks), "sample")
    return parts.reshape(blocks // 2, 2 * kept.shape[0], LANES)


def per_device(energy, coef, anchor, f_start):
    groups = lax.axis_size("state")
    blocks = lax.axis_size("sample")
    group = lax.axis_index("state").astype(jnp.int32).reshape(1)
    own = lax.axis_index("sample").astype(jnp.int32).reshape(1)
    pieces = spread(prepare(group, anchor, energy, blocks, groups), "sample")
    packed = spread(pack(pieces, f_start, coef, groups), "state")
    left, amount = arrange(group, own, pieces)
    parts = None
    weights = None
    for iteration in range(ITERS):
        kept, sent, weights, *rest = sweep(amount, own, packed, left, parts, weights)
        if rest:
            left = rest[0]
        parts = merged(kept, sent, groups, blocks)
    return finish(group, parts, weights, groups).reshape(-1)


def solution(mesh):
    in_specs = (P(None, "sample"), P(None, "state"), P("sample"), P("state"))
    out_specs = P("state")
    return jax.shard_map(
        per_device, mesh=mesh, in_specs=in_specs, out_specs=out_specs, check_vma=False
    )
```

```python
import functools

import jax
import jax.numpy as jnp
from jax import lax
from jax.experimental import pallas as pl
from jax.experimental.pallas import tpu as pltpu
from jax.sharding import PartitionSpec as P

ITERS = 2

LOG2E = 1.4426950408889634
LN2 = 0.6931471805599453
LOW = -1.0e30
SAFE_SUM = 1.0e-25
SAFE_TOP = 1.0e30

LANES = 128
STATE_TILE = 256
ROW_TILE = 416
DEPTH = 128
WEIGHT_AT = 96
SHIFT_AT = 99
LIVE_AT = 102


def split3(value):
    high = value.astype(jnp.bfloat16).astype(jnp.float32)
    rest = value - high
    middle = rest.astype(jnp.bfloat16).astype(jnp.float32)
    low = (rest - middle).astype(jnp.bfloat16).astype(jnp.float32)
    return high, middle, low


def live_rows(group, own, live_slots):
    lane = lax.broadcasted_iota(jnp.int32, (1, LANES), 1)
    tile = group + 16 * lax.shift_right_logical(lane, 3)
    slot = tile * LANES + 8 * own + lax.bitwise_and(lane, 7)
    return slot.astype(jnp.float32) < live_slots


def prepare_kernel(group_ref, anchor_hbm_ref, energy_ref, out_ref, anchor_ref, tile_ref, anchor_sems, sems):
    group = group_ref[0]
    tiles = tile_ref.shape[0]

    def fetch(i):
        at = pl.multiple_of((group + tiles * i) * LANES, LANES)
        return pltpu.make_async_copy(energy_ref.at[:, pl.ds(at, LANES)], tile_ref.at[i], sems.at[i])

    total = anchor_ref.shape[1]
    step = 4096

    def fetch_anchor(k):
        part = pl.ds(k * step, step)
        return pltpu.make_async_copy(anchor_hbm_ref.at[:, part], anchor_ref.at[:, part], anchor_sems.at[k])

    for k in range(total // step):
        fetch_anchor(k).start()
    for i in range(tiles):
        fetch(i).start()
    base = group * 16
    row = lax.broadcasted_iota(jnp.int32, (16, step), 0)
    counts = jnp.zeros((16, 16), jnp.float32)
    live = jnp.zeros((1, step), jnp.float32)
    for start in range(0, total, step):
        fetch_anchor(start // step).wait()
        anchor = anchor_ref[:, start : start + step]
        high = lax.shift_right_logical(anchor, 4) - base
        low = lax.bitwise_and(anchor, 15)
        high_hot = jnp.where(row == high, 1.0, 0.0).astype(jnp.bfloat16)
        low_hot = jnp.where(row == low, 1.0, 0.0).astype(jnp.bfloat16)
        live += jnp.where(anchor < tiles * STATE_TILE, 1.0, 0.0)
        counts += lax.dot_general(
            high_hot, low_hot, (((1,), (1,)), ((), ())), preferred_element_type=jnp.float32
        )
    lane = lax.broadcasted_iota(jnp.int32, (16, 256), 1)
    row16 = lax.broadcasted_iota(jnp.int32, (16, 256), 0)
    spread_out = jnp.where(lax.bitwise_and(lane, 15) == row16, 1.0, 0.0)
    placed = lax.dot_general(
        counts,
        spread_out,
        (((1,), (0,)), ((), ())),
        preferred_element_type=jnp.float32,
        precision=lax.Precision.HIGHEST,
    )
    flat = jnp.sum(jnp.where(lax.shift_right_logical(lane, 4) == row16, placed, 0.0), axis=0, keepdims=True)
    amount = jnp.broadcast_to(jnp.sum(live, axis=1, keepdims=True), (1, LANES))

    def halves(value):
        high = jnp.floor(value * (1.0 / 256.0))
        return high, value - high * 256.0

    flat_high, flat_low = halves(flat)
    rows = [flat_high[:, :LANES], flat_high[:, LANES:], flat_low[:, :LANES], flat_low[:, LANES:]]
    rows += list(halves(amount)) + [jnp.zeros((2, LANES), jnp.float32)]
    for i in range(tiles):
        fetch(i).wait()
    lane = lax.shift_right_logical(lax.broadcasted_iota(jnp.int32, tile_ref.shape[1:], 1), 3)
    energies = [tile_ref[i].astype(jnp.float32) for i in range(tiles)]
    for j in range(out_ref.shape[0]):
        piece = energies[j]
        for i in range(tiles):
            if i != j:
                piece = jnp.where(lane == i, pltpu.roll(energies[i], (8 * (i - j)) % LANES, 1), piece)
        out_ref[j] = jnp.concatenate([piece] + rows, axis=0).astype(jnp.bfloat16)


def prepare(group, anchor, energy, copies, groups):
    total = anchor.shape[0]
    components = energy.shape[0]
    hbm = pltpu.MemorySpace.HBM
    return pl.pallas_call(
        prepare_kernel,
        out_shape=jax.ShapeDtypeStruct((copies, components + 8, LANES), jnp.bfloat16),
        in_specs=[pl.BlockSpec(memory_space=pltpu.SMEM)] + [pl.BlockSpec(memory_space=hbm)] * 2,
        out_specs=pl.BlockSpec(memory_space=pltpu.VMEM),
        scratch_shapes=[
            pltpu.VMEM((1, total), jnp.int32),
            pltpu.VMEM((groups, components, LANES), jnp.bfloat16),
            pltpu.SemaphoreType.DMA((total // 4096,)),
            pltpu.SemaphoreType.DMA((groups,)),
        ],
        compiler_params=pltpu.CompilerParams(vmem_limit_bytes=8 * 2**20),
        name="prepare",
    )(
        group,
        pltpu.with_memory_space_constraint(anchor.reshape(1, total), hbm),
        pltpu.with_memory_space_constraint(energy, hbm),
    )


def arrange_kernel(group_ref, own_ref, pieces_ref, left_ref, amount_ref, wide_ref):
    components = pieces_ref.shape[1] - 8
    wide_ref[...] = jnp.zeros_like(wide_ref)
    lane = lax.broadcasted_iota(jnp.int32, (1, LANES), 1)
    row = lax.broadcasted_iota(jnp.int32, (DEPTH - 3 * components, LANES), 0)
    at = jnp.int32(0)
    for b in range(pieces_ref.shape[0]):
        piece = pieces_ref[b].astype(jnp.float32)
        rest = piece[components:]
        is_live = live_rows(group_ref[0], own_ref[0], rest[4:5] * 256.0 + rest[5:6])
        live = jnp.where(is_live, 1.0, 0.0)
        starts = jnp.where(lax.bitwise_and(lane, 7) == 0, live, 0.0)
        energy = piece[:components] * live
        tail = jnp.where(row < SHIFT_AT - WEIGHT_AT, 1.0, jnp.where(row == LIVE_AT - WEIGHT_AT, live, 0.0))
        block = jnp.concatenate([energy, energy, energy, tail], axis=0)
        wide_ref[pl.ds(pl.multiple_of(at, 8), LANES), :] = block.T
        at = at + 8 * jnp.sum(starts).astype(jnp.int32)
    left_ref[...] = wide_ref[...].astype(jnp.bfloat16)
    amount_ref[0] = at


def arrange(group, own, pieces):
    most = pl.cdiv(pieces.shape[0] * LANES, 2 * ROW_TILE) * 2 * ROW_TILE
    smem = pl.BlockSpec(memory_space=pltpu.SMEM)
    vmem = pl.BlockSpec(memory_space=pltpu.VMEM)
    return pl.pallas_call(
        arrange_kernel,
        out_shape=[
            jax.ShapeDtypeStruct((most, DEPTH), jnp.bfloat16),
            jax.ShapeDtypeStruct((1,), jnp.int32),
        ],
        in_specs=[smem, smem, vmem],
        out_specs=[vmem, smem],
        scratch_shapes=[pltpu.VMEM((most, DEPTH), jnp.float32)],
        compiler_params=pltpu.CompilerParams(vmem_limit_bytes=6 * 2**20),
        name="arrange",
    )(group, own, pieces)


def pack_kernel(pieces_ref, start_ref, coef_ref, out_ref):
    components = coef_ref.shape[0]
    counts = jnp.sum(pieces_ref[:, components:, :].astype(jnp.float32), axis=0)
    counts = jnp.concatenate([counts[0:1], counts[1:2]], axis=1) * 256.0 + jnp.concatenate(
        [counts[2:3], counts[3:4]], axis=1
    )
    rows = list(split3(jnp.log(counts))) + list(split3(start_ref[...]))
    rows.append(jnp.zeros((2, STATE_TILE), jnp.float32))
    packed = jnp.concatenate([coef_ref[...].astype(jnp.float32)] + rows, axis=0).astype(jnp.bfloat16)
    out_ref[...] = jnp.broadcast_to(packed[None], out_ref.shape)


def pack(pieces, f_start, coef, copies):
    components, states = coef.shape
    return pl.pallas_call(
        pack_kernel,
        out_shape=jax.ShapeDtypeStruct((copies, components + 8, states), jnp.bfloat16),
        compiler_params=pltpu.CompilerParams(vmem_limit_bytes=4 * 2**20),
        name="pack",
    )(pieces, f_start.reshape(1, states), coef)


def merge_logs(parts):
    highest = jnp.max(parts, axis=0)
    return highest + jnp.log2(jnp.sum(jnp.exp2(parts - highest[None]), axis=0))


def merge_pair_kernel(kept_ref, other_ref, out_ref):
    kept = kept_ref[...]
    other = other_ref[...]
    highest = jnp.maximum(kept, other)
    value = highest + jnp.log2(jnp.exp2(kept - highest) + jnp.exp2(other - highest))
    out_ref[...] = jnp.broadcast_to(value[None], out_ref.shape)


def merge_pair(kept, other, copies):
    return pl.pallas_call(
        merge_pair_kernel,
        out_shape=jax.ShapeDtypeStruct((copies,) + kept.shape, jnp.float32),
        compiler_params=pltpu.CompilerParams(vmem_limit_bytes=4 * 2**20),
        name="merge_pair",
    )(kept, other)


def merge_kernel(parts_ref, out_ref):
    out_ref[...] = jnp.broadcast_to(merge_logs(parts_ref[...])[None], out_ref.shape)


def merge(parts, copies):
    return pl.pallas_call(
        merge_kernel,
        out_shape=jax.ShapeDtypeStruct((copies,) + parts.shape[1:], jnp.float32),
        compiler_params=pltpu.CompilerParams(vmem_limit_bytes=4 * 2**20),
        name="merge",
    )(parts)


def centered(value):
    mean = jnp.sum(jnp.sum(value, axis=1, keepdims=True), axis=0, keepdims=True) / value.size
    return value - mean


def largest(value):
    return jnp.max(jnp.max(value, axis=1, keepdims=True), axis=0, keepdims=True)


def folded(value, combine):
    return combine(value[:, :LANES], value[:, LANES:])


def sweep_kernel(first, *refs):
    if first:
        amount_ref, own_ref, packed_ref, left_ref, kept_ref, sent_ref, wide_ref, shifted_ref, right_ref, even_ref, odd_ref, even_share_ref, odd_share_ref, acc_ref, some_ref, tall_ref, top_ref = refs
        source_ref = shifted_ref
    else:
        amount_ref, own_ref, packed_ref, left_ref, parts_ref, old_ref, kept_ref, sent_ref, wide_ref, some_ref, right_ref, even_ref, odd_ref, even_share_ref, odd_share_ref, acc_ref, tall_ref, top_ref = refs
        source_ref = left_ref
    scaled_refs = (even_ref, odd_ref)
    share_refs = (even_share_ref, odd_share_ref)
    groups, packed_rows, _ = packed_ref.shape
    components = packed_rows - 8
    states = groups * STATE_TILE
    pair = STATE_TILE // LANES
    amount = amount_ref[0]
    tiles = (amount + ROW_TILE - 1) // ROW_TILE

    for g in range(groups):
        rows = packed_ref[g, components:, :].astype(jnp.float32)
        log_counts = rows[0:1] + rows[1:2] + rows[2:3]
        value = log_counts + (rows[3:4] + rows[4:5] + rows[5:6]) if first else log_counts
        for h in range(pair):
            wide_ref[pair * g + h : pair * g + h + 1, :] = value[:, h * LANES : (h + 1) * LANES]
    if first:
        weights = wide_ref[...]
    else:
        raw = old_ref[...] - merge_logs(parts_ref[...]) * LN2
        wide = wide_ref[...] + centered(raw)
        wide_ref[...] = wide
        weights = wide - largest(wide - old_ref[...])
    w0, w1, w2 = split3(weights * LOG2E)

    row = lax.broadcasted_iota(jnp.int32, (DEPTH - 3 * components, LANES), 0)
    ones = jnp.where(row < LIVE_AT - WEIGHT_AT, 1.0, 0.0)
    for g in range(groups):
        coef = packed_ref[g, :components, :].astype(jnp.float32) * (-LOG2E)
        lanes = slice(g * STATE_TILE, (g + 1) * STATE_TILE)
        for k, part in enumerate(split3(coef)):
            right_ref[k * components : (k + 1) * components, lanes] = part.astype(jnp.bfloat16)
        for h in range(pair):
            at = pair * g + h
            tail = jnp.where(row == 0, w0[at : at + 1], jnp.where(row == 1, w1[at : at + 1], jnp.where(row == 2, w2[at : at + 1], ones)))
            right_ref[WEIGHT_AT:, at * LANES : (at + 1) * LANES] = tail.astype(jnp.bfloat16)

    def product(left, right):
        return lax.dot_general(left, right, (((1,), (0,)), ((), ())), preferred_element_type=jnp.float32)

    if first:
        lane = lax.broadcasted_iota(jnp.int32, (DEPTH, LANES), 1)
        for h in range(2):
            some = jnp.zeros((DEPTH, LANES), jnp.float32)
            for j in range(8):
                g = 8 * h + j
                tile = right_ref[:, g * STATE_TILE : g * STATE_TILE + LANES].astype(jnp.float32)
                moved = tile if j == 0 else pltpu.roll(tile, 16 * j, 1)
                some = jnp.where(lax.shift_right_logical(lane, 4) == j, moved, some)
            some_ref[:, h * LANES : (h + 1) * LANES] = some.astype(jnp.bfloat16)

    acc_ref[...] = jnp.zeros_like(acc_ref)
    lane = lax.broadcasted_iota(jnp.int32, (ROW_TILE, LANES), 1)

    def shifted(block, shift):
        s0, s1, s2 = split3(-shift)
        values = jnp.where(lane == SHIFT_AT, s0, jnp.where(lane == SHIFT_AT + 1, s1, s2))
        chosen = jnp.logical_and(lane >= SHIFT_AT, lane < LIVE_AT)
        return jnp.where(chosen, values, block.astype(jnp.float32)).astype(jnp.bfloat16)

    def begin(t, slot, carry, beside):
        least, most = carry
        rows = pl.ds(pl.multiple_of(t * ROW_TILE, ROW_TILE), ROW_TILE)
        left = left_ref[rows, :]
        if first:
            sampled = folded(product(left, some_ref[...]), jnp.maximum)
            shift = jnp.max(sampled, axis=1, keepdims=True)
            left = shifted(left, shift)
        live = left_ref[rows, LIVE_AT : LIVE_AT + 1].astype(jnp.float32)
        total = jnp.zeros((ROW_TILE, LANES), jnp.float32)
        for g in range(groups):
            lanes = slice(g * STATE_TILE, (g + 1) * STATE_TILE)
            scaled = jnp.exp2(product(left, right_ref[:, lanes]))
            scaled_refs[slot][:, lanes] = scaled
            total += folded(scaled, jnp.add)
            beside(g)
        denominator = jnp.sum(total, axis=1, keepdims=True)
        least = jnp.minimum(least, jnp.where(live > 0.0, denominator, 1.0))
        most = jnp.maximum(most, jnp.where(live > 0.0, denominator, 1.0))
        share_refs[slot][...] = jnp.broadcast_to(live / denominator, (ROW_TILE, LANES))
        if first:
            shifted_ref[rows, :] = shifted(left, shift + jnp.log2(denominator))
        return least, most

    def end(slot, g):
        for h in range(pair):
            lanes = slice((pair * g + h) * LANES, (pair * g + h + 1) * LANES)
            part = scaled_refs[slot][:, lanes] * share_refs[slot][...]
            acc_ref[:, lanes] += jnp.sum(part.reshape(ROW_TILE // 8, 8, LANES), axis=0)

    def visit(t, carry):
        carry = begin(2 * t, 0, carry, lambda g: None)
        carry = begin(2 * t + 1, 1, carry, lambda g: end(0, g))
        for g in range(groups):
            end(1, g)
        return carry

    unit = jnp.ones((ROW_TILE, 1), jnp.float32)
    least, most = lax.fori_loop(0, (tiles + 1) // 2, visit, (unit, unit))
    least = jnp.min(least, axis=0, keepdims=True)
    most = jnp.max(most, axis=0, keepdims=True)
    sums = jnp.sum(acc_ref[...], axis=0, keepdims=True)
    smallest = jnp.min(sums, axis=1, keepdims=True)
    logs = jnp.where(sums > 0.0, jnp.log2(jnp.maximum(sums, SAFE_SUM)), LOW)

    def give(value):
        for k in range(states // LANES):
            tall_ref[k : k + 1, :] = value[:, k * LANES : (k + 1) * LANES]
        half = kept_ref.shape[0]
        core = lax.rem(own_ref[0], 2)
        kept_ref[...] = tall_ref[pl.ds(pl.multiple_of(core * half, half), half), :]
        sent_ref[...] = tall_ref[pl.ds(pl.multiple_of((1 - core) * half, half), half), :]

    give(logs)
    enough = jnp.logical_and(smallest >= SAFE_SUM, smallest * least >= SAFE_SUM)
    safe = jnp.logical_and(enough, jnp.logical_and(most < SAFE_TOP, least > SAFE_SUM))
    unsafe = jnp.max(jnp.where(safe, 0.0, 1.0)) > 0.0

    @pl.when(jnp.logical_and(amount > 0, unsafe))
    def exact():
        acc_ref[...] = jnp.zeros_like(acc_ref)
        top_ref[...] = jnp.full_like(top_ref, LOW)

        def tile_at(k):
            return pl.ds(pl.multiple_of(k * LANES, LANES), LANES)

        def slots(t, carry):
            rows = pl.ds(pl.multiple_of(t * ROW_TILE, ROW_TILE), ROW_TILE)
            left = left_ref[rows, :]
            is_live = jnp.broadcast_to(left[:, LIVE_AT : LIVE_AT + 1].astype(jnp.float32), (ROW_TILE, LANES)) > 0.0

            def column(k, pieces):
                high, total = pieces
                score = product(left, right_ref[:, tile_at(k)])
                newer = jnp.maximum(high, score)
                return newer, total * jnp.exp2(high - newer) + jnp.exp2(score - newer)

            start = (jnp.full((ROW_TILE, LANES), LOW, jnp.float32), jnp.zeros((ROW_TILE, LANES), jnp.float32))
            high, total = lax.fori_loop(0, states // LANES, column, start)
            top = jnp.max(high, axis=1, keepdims=True)
            total = jnp.sum(total * jnp.exp2(high - top), axis=1, keepdims=True)
            norm = top + jnp.log2(total)
            if first:
                shifted_ref[rows, :] = shifted(left, norm)

            def state(k, inner):
                lanes = tile_at(k)
                term = jnp.where(is_live, product(left, right_ref[:, lanes]) - norm, LOW)
                older = top_ref[:, lanes]
                newer = jnp.maximum(older, jnp.max(term, axis=0, keepdims=True))
                added = jnp.sum(jnp.where(is_live, jnp.exp2(term - newer), 0.0), axis=0, keepdims=True)
                acc_ref[0:1, lanes] = acc_ref[0:1, lanes] * jnp.exp2(older - newer) + added
                top_ref[:, lanes] = newer
                return inner

            return lax.fori_loop(0, states // LANES, state, carry)

        lax.fori_loop(0, tiles, slots, 0)
        give(top_ref[...] + jnp.log2(acc_ref[0:1, :]))


def sweep(amount, own, packed, left, parts, old):
    groups = packed.shape[0]
    states = groups * STATE_TILE
    first = parts is None
    tall = states // LANES
    operands = [amount, own, packed, left] + ([] if first else [parts, old])
    outs = [((tall // 2, LANES), jnp.float32)] * 2 + [((tall, LANES), jnp.float32)]
    scratch = [
        pltpu.VMEM((DEPTH, states), jnp.bfloat16),
        pltpu.VMEM((ROW_TILE, states), jnp.float32),
        pltpu.VMEM((ROW_TILE, states), jnp.float32),
        pltpu.VMEM((ROW_TILE, LANES), jnp.float32),
        pltpu.VMEM((ROW_TILE, LANES), jnp.float32),
        pltpu.VMEM((8, states), jnp.float32),
        pltpu.VMEM((DEPTH, 2 * LANES), jnp.bfloat16),
        pltpu.VMEM((tall, LANES), jnp.float32),
        pltpu.VMEM((1, states), jnp.float32),
    ]
    if first:
        outs.append((left.shape, jnp.bfloat16))
    else:
        scratch = [scratch[6]] + scratch[:6] + scratch[7:]
    return pl.pallas_call(
        functools.partial(sweep_kernel, first),
        out_shape=[jax.ShapeDtypeStruct(*out) for out in outs],
        in_specs=[pl.BlockSpec(memory_space=pltpu.SMEM)] * 2 + [pl.BlockSpec(memory_space=pltpu.VMEM)] * (len(operands) - 2),
        scratch_shapes=scratch,
        compiler_params=pltpu.CompilerParams(vmem_limit_bytes=28 * 2**20),
        name="first_sweep" if first else "next_sweep",
    )(*operands)


def finish_kernel(group_ref, parts_ref, old_ref, out_ref, hold_ref):
    raw = old_ref[...] - merge_logs(parts_ref[...]) * LN2
    hold_ref[...] = centered(raw)
    out_ref[...] = hold_ref[pl.ds(group_ref[0] * out_ref.shape[0], out_ref.shape[0]), :]


def finish(group, parts, old, groups):
    rows = old.shape[0] // groups
    return pl.pallas_call(
        finish_kernel,
        out_shape=jax.ShapeDtypeStruct((rows, LANES), jnp.float32),
        grid_spec=pltpu.PrefetchScalarGridSpec(
            num_scalar_prefetch=1,
            grid=(1,),
            in_specs=[
                pl.BlockSpec(parts.shape, lambda i, g: (0, 0, 0)),
                pl.BlockSpec(old.shape, lambda i, g: (0, 0)),
            ],
            out_specs=pl.BlockSpec((rows, LANES), lambda i, g: (0, 0)),
            scratch_shapes=[pltpu.VMEM(old.shape, jnp.float32)],
        ),
        compiler_params=pltpu.CompilerParams(vmem_limit_bytes=4 * 2**20),
        name="finish",
    )(group, parts, old)


def spread(copies, axis):
    return lax.all_to_all(copies, axis, 0, 0)


def merged(kept, sent, groups, blocks):
    other = lax.ppermute(sent, "sample", [(i, i ^ 1) for i in range(blocks)])
    across = spread(merge_pair(kept, other, groups), "state")
    parts = spread(merge(across, blocks), "sample")
    return parts.reshape(blocks // 2, 2 * kept.shape[0], LANES)


def per_device(energy, coef, anchor, f_start):
    groups = lax.axis_size("state")
    blocks = lax.axis_size("sample")
    group = lax.axis_index("state").astype(jnp.int32).reshape(1)
    own = lax.axis_index("sample").astype(jnp.int32).reshape(1)
    pieces = spread(prepare(group, anchor, energy, blocks, groups), "sample")
    packed = spread(pack(pieces, f_start, coef, groups), "state")
    left, amount = arrange(group, own, pieces)
    parts = None
    weights = None
    for iteration in range(ITERS):
        kept, sent, weights, *rest = sweep(amount, own, packed, left, parts, weights)
        if rest:
            left = rest[0]
        parts = merged(kept, sent, groups, blocks)
    return finish(group, parts, weights, groups).reshape(-1)


def solution(mesh):
    in_specs = (P(None, "sample"), P(None, "state"), P("sample"), P("state"))
    out_specs = P("state")
    return jax.shard_map(
        per_device, mesh=mesh, in_specs=in_specs, out_specs=out_specs, check_vma=False
    )
```
